1024 devices in a mesh: vel: 16 (over x_hi, y), space: 64 (over z, x_lo, core).
Axes of the slice: x: 4 (x_hi: 2, x_lo: 2; x = x_hi * 2 + x_lo), y: 8, z: 16, core: 2. Of those that a mesh axis runs over, the one named last changes fastest.
Arguments:
- distribution: float32 [4096, 32768], P('vel', 'space'), may hold values from -6 to 6
- cell_kind: int32 [32768], P('space'), may hold values from 0 to 3
- type_rates: float32 [4], replicated, may hold values from 0.2 to 1
- mode_weights: float32 [512], replicated, may hold values from 0.05 to 1
Outputs:
- result: float32 [4096, 32768], P('vel', 'space')
The draws below stay inside these ranges and needn't reach their ends.
Inputs may be any that keep to these rules, and one draw needn't show every extreme that they name: `cell_kind`: each cell's class.
All inputs are finite; a program needn't handle non-finite values.
Results may differ from the reference program's by a relative error of at most 0.0003.
Values sent between devices are 32-bit elements; how exact they have to be, the bound alone decides.
No kernel may reach another device: no remote copies, remote signals or barrier semaphores. Data moves between devices by JAX's collectives and lax.ppermute only.
A program may use at most 32 MiB of HBM per device.

```python
import math
import jax
import jax.numpy as jnp
from jax import lax

V = 4096
K = 512
STEPS = 2
KINDS = 4
X = 32768


def plant(values, rng, low, high):
    longest = values.shape.index(max(values.shape))
    spots = []
    for shift in (0, 1):
        where = [jax.random.randint(jax.random.fold_in(rng, axis), (), 0, length) for axis, length in enumerate(values.shape)]
        where[longest] = (where[longest] + shift) % values.shape[longest]
        spots.append(tuple(where))
    return values.at[spots[0]].set(low).at[spots[1]].set(high)


def shard_levels(own_key, extent, shards, smallest, largest):
    gain = 1.0
    for position, blocks in shards:
        heights = jax.random.uniform(jax.random.fold_in(jax.random.fold_in(own_key, 6), position), (blocks,), jnp.float32, smallest / len(shards), largest / len(shards))
        gain = gain * jnp.repeat(jnp.exp(heights), extent[position] // blocks).reshape((-1,) + (1,) * (len(extent) - 1 - position))
    return gain


def scatter_about(own_key, dims, deviation, bound, cuts=(), kind=jnp.bfloat16):
    values = jax.random.normal(own_key, dims, jnp.float32) * deviation
    if len(cuts) > 0:
        values = shard_levels(own_key, dims, cuts, -0.22, 0.18) * values
    return jnp.clip(values, min=-bound, max=bound).astype(kind)


def setup_inputs(seed: int = 0) -> dict:
    keys = jax.random.split(jax.random.key(seed), 5)
    distribution = scatter_about(keys[0], (V, X), 1.0, 6.0, ((0, 16), (1, 64)), jnp.float32)
    cell_kind = plant(jax.random.randint(keys[1], (X,), 0, KINDS), jax.random.fold_in(keys[1], 1), 0, KINDS - 1).astype(jnp.int32)
    type_rates = jnp.clip(jax.random.uniform(keys[2], (KINDS,), jnp.float32, 0.2, 1.0), 0.2, 1.0)
    mode_weights = jnp.clip(jnp.exp(jax.random.uniform(keys[3], (K,), jnp.float32, math.log(0.05), math.log(1.0))), 0.05, 1.0)
    return {"distribution": distribution, "cell_kind": cell_kind, "type_rates": type_rates, "mode_weights": mode_weights}


courant_limit = 0.9

def minmod(first_term, second_term):
    lower = jnp.where(first_term > 0.0, jnp.minimum(first_term, second_term), jnp.maximum(first_term, second_term))
    return jnp.where(first_term * second_term > 0.0, lower, jnp.zeros_like(first_term))

def advect(padded, courant):
    width = padded.shape[1] - 4
    differences = padded[:, 1:] - padded[:, :-1]
    slopes = minmod(differences[:, :-1], differences[:, 1:])
    left_face = padded[:, 1:width + 2] + 0.5 * (1.0 - courant) * slopes[:, 0:width + 1]
    right_face = padded[:, 2:width + 3] - 0.5 * (1.0 + courant) * slopes[:, 1:width + 2]
    face_values = jnp.where(courant > 0.0, left_face, right_face)
    return padded[:, 2:width + 2] - courant * (face_values[:, 1:] - face_values[:, :-1])

def courant_numbers(first_velocity, velocity_count):
    velocity_index = first_velocity + jnp.arange(velocity_count, dtype=jnp.int32)
    return ((2 * velocity_index + 1 - V).astype(jnp.float32) * (courant_limit / V))[:, None]

def cosine_factors(first_velocity, velocity_count):
    velocity_index = first_velocity + jnp.arange(velocity_count, dtype=jnp.int32)
    modes = jnp.arange(K, dtype=jnp.int32)
    phase_index = (2 * velocity_index + 1)[:, None] * modes[None, :] % (4 * V)
    phase_angle = phase_index.astype(jnp.float32) * (math.pi / (2 * V))
    column_scale = jnp.where(modes == 0, math.sqrt(1.0 / V), math.sqrt(2.0 / V))
    return jnp.cos(phase_angle) * column_scale[None, :]

def rates_of_cells(cell_kind, type_rates):
    kinds = jnp.arange(type_rates.shape[0], dtype=jnp.int32)
    match = (cell_kind[None, :] == kinds[:, None]).astype(jnp.float32)
    return lax.optimization_barrier(jnp.sum(match * type_rates[:, None], axis=0))

def reference(distribution, cell_kind, type_rates, mode_weights):
    courant = courant_numbers(0, V)
    factors = cosine_factors(0, V)
    cell_rates = rates_of_cells(cell_kind, type_rates)
    vel_block = min(V, 256)
    cell_block = math.gcd(X, 512)
    for time_step in range(STEPS):

        def transport(items):
            rows, numbers = items
            padded = jnp.concatenate([rows[:, -2:], rows, rows[:, :2]], axis=1)
            return advect(padded, numbers)
        advected = lax.map(transport, (distribution.reshape(V // vel_block, vel_block, X), courant.reshape(V // vel_block, vel_block, 1))).reshape(V, X)

        def collide(items):
            cell_columns, rate_block = items
            coefficients = jnp.dot(factors.T, cell_columns, precision=lax.Precision.HIGHEST, preferred_element_type=jnp.float32)
            correction = jnp.dot(factors, mode_weights[:, None] * coefficients, precision=lax.Precision.HIGHEST, preferred_element_type=jnp.float32)
            return cell_columns - rate_block[None, :] * correction
        blocked = advected.reshape(V, X // cell_block, cell_block).transpose(1, 0, 2)
        relaxed = lax.map(collide, (blocked, cell_rates.reshape(X // cell_block, cell_block)))
        distribution = relaxed.transpose(1, 0, 2).reshape(V, X)
    return distribution
```

```python
import functools
import math

import jax
import jax.numpy as jnp
import numpy as np
from jax import lax
from jax.experimental import pallas as pl
from jax.experimental.pallas import tpu as pltpu
from jax.sharding import PartitionSpec as P

V = 4096
K = 512
B = 64
courant_limit = 0.9
F32 = jnp.float32
BF16 = jnp.bfloat16


def tables():
    k = np.arange(K)
    scale = np.where(k == 0, math.sqrt(1.0 / V), math.sqrt(2.0 / V))
    fine = (2 * np.arange(B) + 1)[:, None] * k[None, :] % (4 * V) * (math.pi / (2 * V))
    coarse = (2 * B * np.arange(V // B))[:, None] * k[None, :] % (4 * V) * (math.pi / (2 * V))
    parts = (np.cos(fine) * scale, np.sin(fine) * scale, np.cos(coarse), np.sin(coarse))
    return [part.astype(np.float32) for part in parts]


def split(x):
    hi = x.astype(BF16)
    return hi, (x - hi.astype(F32)).astype(BF16)


def dot(a, b):
    return lax.dot_general(a, b, (((1,), (0,)), ((), ())), preferred_element_type=F32)


def dot_t(a, b):
    return lax.dot_general(a, b, (((1,), (1,)), ((), ())), preferred_element_type=F32)


def minmod(a, b):
    zero = jnp.zeros_like(a)
    return jnp.minimum(jnp.maximum(a, zero), jnp.maximum(b, zero)) + jnp.maximum(
        jnp.minimum(a, zero), jnp.minimum(b, zero)
    )


def advect(padded, courant):
    width = padded.shape[0] - 4
    differences = padded[1:] - padded[:-1]
    slopes = minmod(differences[:-1], differences[1:])
    left_face = padded[1 : width + 2] + 0.5 * (1.0 - courant) * slopes[0 : width + 1]
    right_face = padded[2 : width + 3] - 0.5 * (1.0 + courant) * slopes[1 : width + 2]
    face = jnp.where(courant > 0.0, left_face, right_face)
    return padded[2 : width + 2] - courant * (face[1:] - face[:-1])


def courant_row(first, count):
    v = first + lax.broadcasted_iota(jnp.int32, (1, count), 1)
    return (2 * v + 1 - V).astype(F32) * (courant_limit / V)


def flip_kernel(rates_ref, f_ref, kind_ref, t_ref, first_ref, last_ref):
    kinds = kind_ref[...]
    rate = jnp.zeros(kinds.shape, F32)
    for j in range(rates_ref.shape[1]):
        rate = jnp.where(kinds == j, rates_ref[0, j], rate)
    nv, nx = f_ref.shape
    t_ref[:, :nv] = f_ref[...].T
    t_ref[:, nv:] = jnp.broadcast_to(rate, (128, nx)).T
    first_ref[...] = t_ref[:4, :]
    last_ref[...] = t_ref[nx - 4 :, :]


def factor_kernel(fc_ref, fs_ref, cc_ref, cs_ref, hi_ref, lo_ref):
    def body(a, carry):
        f = fc_ref[...] * cc_ref[pl.ds(a, 1), :] - fs_ref[...] * cs_ref[pl.ds(a, 1), :]
        hi, lo = split(f)
        rows = pl.ds(pl.multiple_of(a * B, B), B)
        hi_ref[rows, :] = hi
        lo_ref[rows, :] = lo
        return carry

    lax.fori_loop(0, V // B, body, 0)


def step_kernel(blocks, t_ref, low_ref, high_ref, out_ref, rate_ref, ext):
    me = lax.axis_index("vel")
    nx = t_ref.shape[0]
    nv = t_ref.shape[1] - 128
    own = nx // blocks
    wide = own + 4
    ext[:4, :] = low_ref[...]
    ext[4 : nx + 4, :] = t_ref[...]
    ext[nx + 4 :, :] = high_ref[...]
    rate_ref[...] = ext[pl.ds(pl.multiple_of(me * own, own), own + 8), nv:][2 : own + 6]
    courant = courant_row(me * nv, nv)
    for j in range(blocks):
        new = advect(ext[j * own : j * own + own + 8, :nv], courant)
        for h in range(nv // 128):
            out_ref[j, h * wide : (h + 1) * wide, :] = new[:, h * 128 : (h + 1) * 128]


def collide_kernel(g_ref, rate_ref, w_ref, hi_ref, lo_ref, out_ref, a_ref, l_ref, c_ref, m_ref):
    blocks = g_ref.shape[0]
    wide = g_ref.shape[1] // 2
    own = wide - 4
    nv = V // blocks
    pad = 48

    def put(columns, value, at):
        hi, lo = split(value)
        rows = value.shape[0]
        l_ref[0:rows, columns] = hi
        l_ref[at : at + rows, columns] = lo

    def correction(rows, at):
        left = l_ref[: 2 * at, :]
        both = dot(left, hi_ref[...])
        coef = both[:rows] + both[at : at + rows] + dot(left[:at], lo_ref[...])[:rows]
        hi, lo = split(coef * w_ref[...])
        m_ref[0:rows, :] = hi
        m_ref[at : at + rows, :] = lo
        right = m_ref[: 2 * at, :]
        c_ref[: 2 * at, :] = dot_t(right, hi_ref[...])
        c_ref[:at, :] += dot_t(right[:at], lo_ref[...])

    for i in range(blocks):
        for h in range(nv // 128):
            part = g_ref[i, h * wide : (h + 1) * wide, :]
            columns = slice(i * nv + h * 128, i * nv + (h + 1) * 128)
            a_ref[:wide, columns] = part
            put(columns, part, pad)
    correction(wide, pad)
    rate = rate_ref[...]
    for i in range(V // 128):
        columns = slice(i * 128, (i + 1) * 128)
        f = a_ref[:wide, columns] - rate * (c_ref[0:wide, columns] + c_ref[pad : pad + wide, columns])
        new = advect(f, courant_row(i * 128, 128))
        a_ref[:own, columns] = new
        put(columns, new, own)
    correction(own, own)
    rate = rate[2 : own + 2]
    for i in range(V // 128):
        columns = slice(i * 128, (i + 1) * 128)
        f = a_ref[:own, columns] - rate * (c_ref[0:own, columns] + c_ref[own : 2 * own, columns])
        j = i * 128 // nv
        out_ref[j, :, i * 128 - j * nv : i * 128 - j * nv + 128] = f


def unflip_kernel(t_ref, out_ref):
    out_ref[...] = t_ref[...].T


def params(mib):
    return pltpu.CompilerParams(vmem_limit_bytes=mib * 1024 * 1024)


def vmem(count):
    return [pl.BlockSpec(memory_space=pltpu.VMEM)] * count


def shards(distribution, cell_kind, type_rates, mode_weights):
    nv, nx = distribution.shape
    blocks = lax.axis_size("vel")
    slabs = lax.axis_size("space")
    own = nx // blocks
    forward = [(i, (i + 1) % slabs) for i in range(slabs)]
    backward = [(target, source) for source, target in forward]
    turned, first, last = pl.pallas_call(
        flip_kernel,
        out_shape=(
            jax.ShapeDtypeStruct((nx, nv + 128), F32),
            jax.ShapeDtypeStruct((4, nv + 128), F32),
            jax.ShapeDtypeStruct((4, nv + 128), F32),
        ),
        in_specs=[pl.BlockSpec(memory_space=pltpu.SMEM)] + vmem(2),
        out_specs=tuple(vmem(3)),
        compiler_params=params(8),
        name="flip",
    )(type_rates[None, :], distribution, cell_kind[None, :])
    low = lax.ppermute(last, "space", forward)
    high = lax.ppermute(first, "space", backward)
    fhi, flo = pl.pallas_call(
        factor_kernel,
        out_shape=(jax.ShapeDtypeStruct((V, K), BF16), jax.ShapeDtypeStruct((V, K), BF16)),
        in_specs=vmem(4),
        out_specs=tuple(vmem(2)),
        compiler_params=params(12),
        name="factors",
    )(*[jnp.asarray(t) for t in tables()])
    sent, rate = pl.pallas_call(
        functools.partial(step_kernel, blocks),
        out_shape=(
            jax.ShapeDtypeStruct((blocks, 2 * (own + 4), nv // 2), F32),
            jax.ShapeDtypeStruct((own + 4, 128), F32),
        ),
        in_specs=vmem(3),
        out_specs=tuple(vmem(2)),
        scratch_shapes=[pltpu.VMEM((nx + 8, nv + 128), F32)],
        compiler_params=params(8),
        name="transport",
    )(turned, low, high)
    got = lax.all_to_all(sent, "vel", 0, 0, tiled=True)
    back = pl.pallas_call(
        collide_kernel,
        out_shape=jax.ShapeDtypeStruct((blocks, own, nv), F32),
        in_specs=vmem(5),
        out_specs=pl.BlockSpec(memory_space=pltpu.VMEM),
        scratch_shapes=[
            pltpu.VMEM((40, V), F32),
            pltpu.VMEM((96, V), BF16),
            pltpu.VMEM((96, V), F32),
            pltpu.VMEM((96, K), BF16),
        ],
        compiler_params=params(24),
        name="collide",
    )(got, rate, mode_weights[None, :], fhi, flo)
    result = lax.all_to_all(back, "vel", 0, 0, tiled=True)
    return pl.pallas_call(
        unflip_kernel,
        out_shape=jax.ShapeDtypeStruct((nv, nx), F32),
        in_specs=vmem(1),
        out_specs=pl.BlockSpec(memory_space=pltpu.VMEM),
        compiler_params=params(8),
        name="unflip",
    )(result.reshape(nx, nv))


def solution(mesh):
    return jax.shard_map(
        shards,
        mesh=mesh,
        in_specs=(P("vel", "space"), P("space"), P(), P()),
        out_specs=P("vel", "space"),
        check_vma=False,
    )
```

```python
import functools
import math

import jax
import jax.numpy as jnp
import numpy as np
from jax import lax
from jax.experimental import pallas as pl
from jax.experimental.pallas import tpu as pltpu
from jax.sharding import PartitionSpec as P

V = 4096
K = 512
H = V // 2
B = 64
A = H // B
LANES = 256
courant_limit = 0.9
F32 = jnp.float32
BF16 = jnp.bfloat16


def tables():
    k = np.concatenate([np.arange(0, K, 2), np.arange(1, K, 2)])
    scale = np.where(k == 0, math.sqrt(1.0 / V), math.sqrt(2.0 / V))
    fine = (2 * np.arange(B) + 1)[:, None] * k[None, :] % (4 * V) * (math.pi / (2 * V))
    coarse = (2 * B * np.arange(A))[:, None] * k[None, :] % (4 * V) * (math.pi / (2 * V))
    parts = (np.cos(fine) * scale, np.sin(fine) * scale, np.cos(coarse), np.sin(coarse))
    return np.concatenate(parts).astype(np.float32)


def window_of(rank, blocks):
    return [0, blocks - 1][rank] if rank < 2 else rank - 1


def split(x):
    hi = x.astype(BF16)
    return hi, (x - hi.astype(F32)).astype(BF16)


def dot(a, b):
    return lax.dot_general(a, b, (((1,), (0,)), ((), ())), preferred_element_type=F32)


def dot_t(a, b):
    return lax.dot_general(a, b, (((1,), (1,)), ((), ())), preferred_element_type=F32)


def exact_dot(x, picks):
    hi = x.astype(BF16)
    rest = x - hi.astype(F32)
    mid = rest.astype(BF16)
    low = (rest - mid.astype(F32)).astype(BF16)
    return dot(hi, picks) + (dot(mid, picks) + dot(low, picks))


def minmod(a, b):
    zero = jnp.zeros_like(a)
    return jnp.minimum(jnp.maximum(a, zero), jnp.maximum(b, zero)) + jnp.maximum(
        jnp.minimum(a, zero), jnp.minimum(b, zero)
    )


def advect(padded, courant, positive):
    width = padded.shape[0] - 4
    differences = padded[1:] - padded[:-1]
    slopes = minmod(differences[:-1], differences[1:])
    if positive:
        face = padded[1 : width + 2] + 0.5 * (1.0 - courant) * slopes[0 : width + 1]
    else:
        face = padded[2 : width + 3] - 0.5 * (1.0 + courant) * slopes[1 : width + 2]
    return padded[2 : width + 2] - courant * (face[1:] - face[:-1])


def courant_row(velocity):
    return (2 * velocity + 1 - V).astype(F32) * (courant_limit / V)


def flip_kernel(blocks, rates_ref, kind_ref, f_hbm, out_ref, rate_ref, f_ref, ext, rates_ext, sems):
    me = lax.axis_index("vel")
    nv, nx = f_ref.shape
    own = nx // blocks
    parts = nx // 128
    copies = [
        pltpu.make_async_copy(
            f_hbm.at[:, p * 128 : (p + 1) * 128], f_ref.at[:, p * 128 : (p + 1) * 128], sems.at[p]
        )
        for p in range(parts)
    ]
    for copy in copies:
        copy.start()
    kinds = kind_ref[...]
    rate = jnp.zeros(kinds.shape, F32)
    for j in range(rates_ref.shape[1]):
        rate = jnp.where(kinds == j, rates_ref[0, j], rate)
    rates_ext[8 : nx + 8, :] = jnp.broadcast_to(rate, (128, nx)).T
    rates_ext[0:8, :] = jnp.zeros((8, 128), F32)
    rates_ext[nx + 8 :, :] = jnp.zeros((8, 128), F32)
    spot = jnp.where(me == 0, 0, jnp.where(me == 1, blocks - 1, me - 1))
    rate_ref[...] = rates_ext[pl.ds(pl.multiple_of(spot * own, own), own + 16), :][4 : own + 12]
    for p in range(parts):
        copies[p].wait()
        ext[8 + p * 128 : 8 + (p + 1) * 128, :] = f_ref[:, p * 128 : (p + 1) * 128].T
    first = rates_ext[8:12, :]
    last = rates_ext[nx + 4 : nx + 8, :]
    for h in range(nv // 128):
        ext[4:8, h * 128 : (h + 1) * 128] = first
        ext[nx + 8 : nx + 12, h * 128 : (h + 1) * 128] = last
    for r in range(blocks):
        at = 4 + window_of(r, blocks) * own
        out_ref[r] = ext[at : at + own + 8, :]


def factor_kernel(table_hbm, w_ref, edge_hbm, hi_ref, lo_ref, wp_ref, table, sem):
    copy = pltpu.make_async_copy(table_hbm, table, sem)
    copy.start()
    source = lax.broadcasted_iota(jnp.int32, (K, K), 0)
    target = lax.broadcasted_iota(jnp.int32, (K, K), 1)
    mode = jnp.where(target < K // 2, 2 * target, 2 * target + 1 - K)
    picks = jnp.where(source == mode, 1.0, 0.0).astype(BF16)
    wp_ref[...] = exact_dot(jnp.broadcast_to(w_ref[...], (8, K)), picks)
    copy.wait()

    def body(a, carry):
        f = table[0:B, :] * table[pl.ds(2 * B + a, 1), :] - table[B : 2 * B, :] * table[pl.ds(2 * B + A + a, 1), :]
        hi, lo = split(f)
        rows = pl.ds(pl.multiple_of(a * B, B), B)
        hi_ref[rows, :] = hi
        lo_ref[rows, :] = lo
        return carry

    lax.fori_loop(0, A, body, 0)


def collide_kernel(g_ref, e_ref, rate_in, wp_ref, hi_ref, lo_ref, out_ref, a_ref, b_ref, r_ref, l_ref, c_ref, m_ref):
    me = lax.axis_index("vel")
    blocks, window, nv = g_ref.shape
    own = window - 8
    wide = window - 4
    pad = 48
    half = K // 2
    lower = [slice(c * LANES, (c + 1) * LANES) for c in range(H // LANES)]
    upper = [slice(H + c * LANES, H + (c + 1) * LANES) for c in range(H // LANES)]
    lane = lax.broadcasted_iota(jnp.int32, (1, LANES), 1)
    turn = jnp.where(
        lax.broadcasted_iota(jnp.int32, (LANES, LANES), 0)
        + lax.broadcasted_iota(jnp.int32, (LANES, LANES), 1)
        == LANES - 1,
        1.0,
        0.0,
    ).astype(BF16)

    for i in range(blocks):
        a_ref[:, i * nv : (i + 1) * nv] = g_ref[i]
    r_ref[...] = rate_in[...]

    @pl.when(me == 0)
    def _():
        for i in range(blocks):
            a_ref[0:4, i * nv : (i + 1) * nv] = e_ref[i, 0:4, :]
        r_ref[0:4, :] = e_ref[0, 4:8, :128]

    @pl.when(me == 1)
    def _():
        for i in range(blocks):
            a_ref[window - 4 :, i * nv : (i + 1) * nv] = e_ref[i, 4:8, :]
        r_ref[window - 4 :, :] = e_ref[0, 0:4, :128]

    def fold(c, up, down, at):
        rows = up.shape[0]
        for part, columns in ((up + down, lower[c]), (up - down, upper[c])):
            hi, lo = split(part)
            l_ref[0:rows, columns] = hi
            l_ref[at : at + rows, columns] = lo

    def correction(rows, at):
        for s in range(2):
            modes = slice(s * half, (s + 1) * half)
            left = l_ref[: 2 * at, s * H : (s + 1) * H]
            both = dot(left, hi_ref[:, modes])
            coef = both[:rows] + both[at : at + rows] + dot(left[:at], lo_ref[:, modes])[:rows]
            hi, lo = split(coef * wp_ref[0:1, modes])
            m_ref[0:rows, modes] = hi
            m_ref[at : at + rows, modes] = lo
            right = m_ref[: 2 * at, modes]
            back = dot_t(right, hi_ref[:, modes])
            c_ref[:rows, s * H : (s + 1) * H] = (
                back[:rows] + back[at : at + rows] + dot_t(right[:at], lo_ref[:, modes])[:rows]
            )

    def courants(c):
        v = lane + c * LANES
        return courant_row(v), courant_row(V - 1 - v)

    def mirror(c):
        return slice(V - (c + 1) * LANES, V - c * LANES)

    for c in range(H // LANES):
        down, up = courants(c)
        new = advect(a_ref[:, lower[c]], down, False)
        turned = advect(exact_dot(a_ref[:, mirror(c)], turn), up, True)
        b_ref[:wide, lower[c]] = new
        b_ref[:wide, upper[c]] = turned
        fold(c, new, turned, pad)
    correction(wide, pad)
    rate = jnp.concatenate([r_ref[2 : wide + 2, :]] * (LANES // 128), axis=1)
    for c in range(H // LANES):
        down, up = courants(c)
        even, odd = c_ref[:wide, lower[c]], c_ref[:wide, upper[c]]
        new = advect(b_ref[:wide, lower[c]] - rate * (even + odd), down, False)
        turned = advect(b_ref[:wide, upper[c]] - rate * (even - odd), up, True)
        b_ref[:own, lower[c]] = new
        b_ref[:own, upper[c]] = turned
        fold(c, new, turned, own)
    correction(own, own)
    rate = rate[2 : own + 2]
    for c in range(H // LANES):
        even, odd = c_ref[:own, lower[c]], c_ref[:own, upper[c]]
        out_ref[c] = b_ref[:own, lower[c]] - rate * (even + odd)
        out_ref[blocks - 1 - c] = exact_dot(b_ref[:own, upper[c]] - rate * (even - odd), turn)


def unflip_kernel(t_ref, out_ref):
    blocks, own, _ = t_ref.shape
    order = sorted(range(blocks), key=lambda r: window_of(r, blocks))
    per = 128 // own
    for p in range(blocks // per):
        rows = jnp.concatenate([t_ref[r] for r in order[p * per : (p + 1) * per]], axis=0)
        out_ref[:, p * 128 : (p + 1) * 128] = rows.T


def params(mib):
    return pltpu.CompilerParams(vmem_limit_bytes=mib * 1024 * 1024)


VMEM = pl.BlockSpec(memory_space=pltpu.VMEM)
SMEM = pl.BlockSpec(memory_space=pltpu.SMEM)
ANY = pl.BlockSpec(memory_space=pl.ANY)


def shards(distribution, cell_kind, type_rates, mode_weights):
    nv, nx = distribution.shape
    blocks = lax.axis_size("vel")
    slabs = lax.axis_size("space")
    own = nx // blocks
    window = own + 8
    sent, rate = pl.pallas_call(
        functools.partial(flip_kernel, blocks),
        out_shape=(
            jax.ShapeDtypeStruct((blocks, window, nv), F32),
            jax.ShapeDtypeStruct((window, 128), F32),
        ),
        in_specs=[SMEM, VMEM, ANY],
        out_specs=(VMEM, VMEM),
        scratch_shapes=[
            pltpu.VMEM((nv, nx), F32),
            pltpu.VMEM((nx + 16, nv), F32),
            pltpu.VMEM((nx + 16, 128), F32),
            pltpu.SemaphoreType.DMA((nx // 128,)),
        ],
        compiler_params=params(8),
        name="flip",
    )(type_rates[None, :], cell_kind[None, :], distribution)
    got = lax.all_to_all(sent, "vel", 0, 0, tiled=True)
    me = lax.axis_index("vel")
    edge = lax.dynamic_slice_in_dim(got, jnp.where(me == 0, 0, window - 8), 8, axis=1)
    pairs = []
    for s in range(slabs):
        after = (s + 1) % slabs
        pairs += [(slabs + s, after), (after, slabs + s)]
    edge_in = lax.ppermute(edge, ("vel", "space"), pairs)
    hi, lo, weights = pl.pallas_call(
        factor_kernel,
        out_shape=(
            jax.ShapeDtypeStruct((H, K), BF16),
            jax.ShapeDtypeStruct((H, K), BF16),
            jax.ShapeDtypeStruct((8, K), F32),
        ),
        in_specs=[ANY, VMEM, ANY],
        out_specs=(VMEM, VMEM, VMEM),
        scratch_shapes=[pltpu.VMEM((2 * (A + B), K), F32), pltpu.SemaphoreType.DMA],
        compiler_params=params(12),
        name="factors",
    )(jnp.asarray(tables()), mode_weights[None, :], edge)
    back = pl.pallas_call(
        collide_kernel,
        out_shape=jax.ShapeDtypeStruct((blocks, own, nv), F32),
        in_specs=[VMEM] * 6,
        out_specs=VMEM,
        scratch_shapes=[
            pltpu.VMEM((window, V), F32),
            pltpu.VMEM((window, V), F32),
            pltpu.VMEM((window, 128), F32),
            pltpu.VMEM((96, V), BF16),
            pltpu.VMEM((window, V), F32),
            pltpu.VMEM((96, K), BF16),
        ],
        compiler_params=params(24),
        name="collide",
    )(got, edge_in, rate, weights, hi, lo)
    result = lax.all_to_all(back, "vel", 0, 0, tiled=True)
    return pl.pallas_call(
        unflip_kernel,
        out_shape=jax.ShapeDtypeStruct((nv, nx), F32),
        in_specs=[VMEM],
        out_specs=VMEM,
        compiler_params=params(8),
        name="unflip",
    )(result)


def solution(mesh):
    return jax.shard_map(
        shards,
        mesh=mesh,
        in_specs=(P("vel", "space"), P("space"), P(), P()),
        out_specs=P("vel", "space"),
        check_vma=False,
    )
```

```python
import functools
import math

import jax
import jax.numpy as jnp
import numpy as np
from jax import lax
from jax.experimental import pallas as pl
from jax.experimental.pallas import tpu as pltpu
from jax.sharding import PartitionSpec as P

V = 4096
K = 512
H = V // 2
B = 64
A = H // B
courant_limit = 0.9
F32 = jnp.float32
BF16 = jnp.bfloat16


def tables():
    k = np.concatenate([np.arange(0, K, 2), np.arange(1, K, 2)])
    scale = np.where(k == 0, math.sqrt(1.0 / V), math.sqrt(2.0 / V))
    fine = (2 * np.arange(B) + 1)[:, None] * k[None, :] % (4 * V) * (math.pi / (2 * V))
    coarse = (2 * B * np.arange(A))[:, None] * k[None, :] % (4 * V) * (math.pi / (2 * V))
    parts = (np.cos(fine) * scale, np.sin(fine) * scale, np.cos(coarse), np.sin(coarse))
    return np.concatenate(parts).astype(np.float32)


def split(x):
    hi = x.astype(BF16)
    return hi, (x - hi.astype(F32)).astype(BF16)


def dot(a, b):
    return lax.dot_general(a, b, (((1,), (0,)), ((), ())), preferred_element_type=F32)


def dot_t(a, b):
    return lax.dot_general(a, b, (((1,), (1,)), ((), ())), preferred_element_type=F32)


def exact_dot(x, picks):
    hi = x.astype(BF16)
    rest = x - hi.astype(F32)
    mid = rest.astype(BF16)
    low = (rest - mid.astype(F32)).astype(BF16)
    return dot(hi, picks) + (dot(mid, picks) + dot(low, picks))


def minmod(a, b):
    zero = jnp.zeros_like(a)
    return jnp.minimum(jnp.maximum(a, zero), jnp.maximum(b, zero)) + jnp.maximum(
        jnp.minimum(a, zero), jnp.minimum(b, zero)
    )


def upwind(far, near, here, other, speed):
    first = near - far
    second = here - near
    change = minmod(second, other - here) - minmod(first, second)
    return here - speed * (second + 0.5 * (1.0 - speed) * change)


def advect(at, speed, positive):
    if positive:
        return upwind(at(-2), at(-1), at(0), at(1), speed)
    return upwind(at(2), at(1), at(0), at(-1), speed)


def courant_row(velocity):
    return (2 * velocity + 1 - V).astype(F32) * (courant_limit / V)


def mirrored(x):
    lane = lax.broadcasted_iota(jnp.int32, x.shape, 1)
    return jnp.take_along_axis(x, 127 - lane, axis=1)


def place(blocks):
    me = lax.axis_index("vel")
    odd = lax.rem(lax.axis_index("space"), 2)
    return jnp.where(me > 1, me - 1, jnp.where(me == odd, 0, blocks - 1))


def flip_kernel(blocks, f_hbm, out_ref, f_ref, ext, sems):
    me = lax.axis_index("vel")
    odd = lax.rem(lax.axis_index("space"), 2)
    nv, nx = f_ref.shape
    own = nx // blocks
    wide = own + 4
    parts = nx // 128
    copies = [
        pltpu.make_async_copy(
            f_hbm.at[:, p * 128 : (p + 1) * 128], f_ref.at[:, p * 128 : (p + 1) * 128], sems.at[p]
        )
        for p in range(parts)
    ]
    for copy in copies:
        copy.start()
    lane = lax.broadcasted_iota(jnp.int32, (1, 128), 1)
    ahead = me >= blocks // 2
    speeds = [jnp.abs(courant_row(me * nv + h * 128 + lane)) for h in range(nv // 128)]

    def make(p, r):
        for h in range(nv // 128):
            base = 8 + p * own - 2

            def at(k, base=base, h=h):
                return ext[h, base + k : base + k + wide, :]

            below, above = at(-1), at(1)
            near = jnp.where(ahead, below, above)
            other = jnp.where(ahead, above, below)
            far = jnp.where(ahead, at(-2), at(2))
            out_ref[r, h * wide : (h + 1) * wide, :] = upwind(far, near, at(0), other, speeds[h])
            if p == 0:
                out_ref[r, h * wide : h * wide + 4, :] = ext[h, 8:12, :]
            if p == blocks - 1:
                out_ref[r, h * wide + own : (h + 1) * wide, :] = ext[h, nx + 4 : nx + 8, :]

    done = 0
    for p in range(parts):
        copies[p].wait()
        for h in range(nv // 128):
            ext[h, 8 + p * 128 : 8 + (p + 1) * 128, :] = f_ref[
                h * 128 : (h + 1) * 128, p * 128 : (p + 1) * 128
            ].T
        while done < blocks and (done == 0 or (done + 1) * own + 4 <= (p + 1) * 128 or p == parts - 1):
            make(done, odd if done == 0 else 1 - odd if done == blocks - 1 else done + 1)
            done += 1


def rate_kernel(blocks, rates_ref, kind_ref, rate_ref, edge_ref, ext):
    nx = kind_ref.shape[1]
    own = nx // blocks
    kinds = kind_ref[...]
    rate = jnp.zeros(kinds.shape, F32)
    for j in range(rates_ref.shape[1]):
        rate = jnp.where(kinds == j, rates_ref[0, j], rate)
    ext[0:8, :] = jnp.zeros((8, 128), F32)
    ext[8 : nx + 8, :] = jnp.broadcast_to(rate, (128, nx)).T
    ext[nx + 8 :, :] = jnp.zeros((8, 128), F32)
    spot = place(blocks)
    rate_ref[...] = ext[pl.ds(pl.multiple_of(spot * own, own), own + 16), :][6 : own + 10]
    edge_ref[...] = jnp.where(spot == 0, ext[8:16, :], ext[nx + 4 : nx + 12, :])


def edge_kernel(g_ref, rate_ref, out_ref):
    blocks, rows, _ = g_ref.shape
    wide = rows // 2
    first = place(blocks) == 0
    for i in range(blocks):
        for h in range(2):
            n = 8 * i + 4 * h
            out_ref[n : n + 4, :] = jnp.where(
                first,
                g_ref[i, h * wide : h * wide + 4, :],
                g_ref[i, (h + 1) * wide - 4 : (h + 1) * wide, :],
            )
    out_ref[8 * blocks :, :] = rate_ref[...]


def factor_kernel(table_hbm, w_ref, edge_hbm, hi_ref, lo_ref, wp_ref, table, sem):
    copy = pltpu.make_async_copy(table_hbm, table, sem)
    copy.start()
    source = lax.broadcasted_iota(jnp.int32, (K, K), 0)
    target = lax.broadcasted_iota(jnp.int32, (K, K), 1)
    mode = jnp.where(target < K // 2, 2 * target, 2 * target + 1 - K)
    picks = jnp.where(source == mode, 1.0, 0.0).astype(BF16)
    wp_ref[...] = exact_dot(jnp.broadcast_to(w_ref[...], (8, K)), picks)
    copy.wait()

    def body(a, carry):
        f = table[0:B, :] * table[pl.ds(2 * B + a, 1), :] - table[B : 2 * B, :] * table[pl.ds(2 * B + A + a, 1), :]
        hi, lo = split(f)
        rows = pl.ds(pl.multiple_of(a * B, B), B)
        hi_ref[rows, :] = hi
        lo_ref[rows, :] = lo
        return carry

    lax.fori_loop(0, A, body, 0)


def collide_kernel(g_ref, e_ref, rate_in, wp_ref, hi_ref, lo_ref, out_ref, a_ref, b_ref, r_ref, l_ref, c_ref, m_ref, s_ref):
    blocks, rows, _ = g_ref.shape
    wide = rows // 2
    own = wide - 4
    pad = 48
    half = K // 2
    chunks = H // 128
    lane = lax.broadcasted_iota(jnp.int32, (1, 128), 1)
    spot = place(blocks)
    r_ref[...] = rate_in[...]

    def given(n):
        return g_ref[n // 2, (n % 2) * wide : (n % 2 + 1) * wide, :]

    for n in range(2 * chunks):
        b_ref[n, 0:wide, :] = given(n)

    def outer(first):
        for n in range(2 * chunks):
            mine = b_ref[n, 0:4, :] if first else b_ref[n, own:wide, :]
            other = e_ref[4 * n : 4 * n + 4, :]
            s_ref[n, 0:4, :] = other if first else mine
            s_ref[n, 4:8, :] = mine if first else other
            speed = jnp.abs(courant_row(lane + n * 128))
            new = advect(lambda k: s_ref[n, 2 + k : 6 + k, :], speed, n >= chunks)
            if first:
                b_ref[n, 0:4, :] = new
            else:
                b_ref[n, own:wide, :] = new
        if first:
            r_ref[0:2, :] = e_ref[8 * blocks + 2 : 8 * blocks + 4, :]
        else:
            r_ref[own + 2 : wide, :] = e_ref[8 * blocks : 8 * blocks + 2, :]

    @pl.when(spot == 0)
    def _():
        outer(True)

    @pl.when(spot == blocks - 1)
    def _():
        outer(False)

    def fold(c, up, down, at):
        count = up.shape[0]
        for part, first in ((up + down, c * 128), (up - down, H + c * 128)):
            hi, lo = split(part)
            l_ref[0:count, first : first + 128] = hi
            l_ref[at : at + count, first : first + 128] = lo

    def correction(count, at):
        for s in range(2):
            modes = slice(s * half, (s + 1) * half)
            left = l_ref[: 2 * at, s * H : (s + 1) * H]
            both = dot(left, hi_ref[:, modes])
            coef = both[:count] + both[at : at + count] + dot(left[:at], lo_ref[:, modes])[:count]
            hi, lo = split(coef * wp_ref[0:1, modes])
            m_ref[0:count, modes] = hi
            m_ref[at : at + count, modes] = lo
            right = m_ref[: 2 * at, modes]
            back = dot_t(right, hi_ref[:, modes])
            c_ref[:count, s * H : (s + 1) * H] = (
                back[:count] + back[at : at + count] + dot_t(right[:at], lo_ref[:, modes])[:count]
            )

    def corrections(count, c):
        even = c_ref[:count, c * 128 : (c + 1) * 128]
        odd = c_ref[:count, H + c * 128 : H + (c + 1) * 128]
        return even + odd, even - odd

    for c in range(chunks):
        down = mirrored(b_ref[2 * chunks - 1 - c, 0:wide, :])
        a_ref[chunks + c, 0:wide, :] = down
        fold(c, b_ref[c, 0:wide, :], down, pad)
    correction(wide, pad)
    rate = r_ref[...]
    for c in range(chunks):
        plus, minus = corrections(wide, c)
        a_ref[c, 0:wide, :] = b_ref[c, 0:wide, :] - rate * plus
        a_ref[chunks + c, 0:wide, :] = a_ref[chunks + c, 0:wide, :] - rate * minus
        speed = jnp.abs(courant_row(lane + c * 128))
        up = advect(lambda k: a_ref[c, 2 + k : 2 + k + own, :], speed, False)
        down = advect(lambda k: a_ref[chunks + c, 2 + k : 2 + k + own, :], speed, True)
        b_ref[c, 0:own, :] = up
        b_ref[chunks + c, 0:own, :] = down
        fold(c, up, down, own)
    correction(own, own)
    rate = r_ref[2 : own + 2, :]
    for c in range(chunks):
        plus, minus = corrections(own, c)
        n = 2 * chunks - 1 - c
        out_ref[c // 2, :, (c % 2) * 128 : (c % 2 + 1) * 128] = b_ref[c, 0:own, :] - rate * plus
        out_ref[n // 2, :, (n % 2) * 128 : (n % 2 + 1) * 128] = mirrored(
            b_ref[chunks + c, 0:own, :] - rate * minus
        )


def unflip_kernel(t_ref, out_ref):
    blocks, own, _ = t_ref.shape
    odd = lax.rem(lax.axis_index("space"), 2)
    order = [odd] + [p + 1 for p in range(1, blocks - 1)] + [1 - odd]
    per = 128 // own
    for p in range(blocks // per):
        rows = jnp.concatenate([t_ref[r] for r in order[p * per : (p + 1) * per]], axis=0)
        out_ref[:, p * 128 : (p + 1) * 128] = rows.T


def params(mib):
    return pltpu.CompilerParams(vmem_limit_bytes=mib * 1024 * 1024)


VMEM = pl.BlockSpec(memory_space=pltpu.VMEM)
SMEM = pl.BlockSpec(memory_space=pltpu.SMEM)
ANY = pl.BlockSpec(memory_space=pl.ANY)


def shards(distribution, cell_kind, type_rates, mode_weights):
    nv, nx = distribution.shape
    blocks = lax.axis_size("vel")
    slabs = lax.axis_size("space")
    own = nx // blocks
    wide = own + 4
    sent = pl.pallas_call(
        functools.partial(flip_kernel, blocks),
        out_shape=jax.ShapeDtypeStruct((blocks, nv // 128 * wide, 128), F32),
        in_specs=[ANY],
        out_specs=VMEM,
        scratch_shapes=[
            pltpu.VMEM((nv, nx), F32),
            pltpu.VMEM((nv // 128, nx + 16, 128), F32),
            pltpu.SemaphoreType.DMA((nx // 128,)),
        ],
        compiler_params=params(8),
        name="flip",
    )(distribution)
    got = lax.all_to_all(sent, "vel", 0, 0, tiled=True)
    rate, rate_edge = pl.pallas_call(
        functools.partial(rate_kernel, blocks),
        out_shape=(
            jax.ShapeDtypeStruct((wide, 128), F32),
            jax.ShapeDtypeStruct((8, 128), F32),
        ),
        in_specs=[SMEM, VMEM],
        out_specs=(VMEM, VMEM),
        scratch_shapes=[pltpu.VMEM((nx + 16, 128), F32)],
        compiler_params=params(8),
        name="rates",
    )(type_rates[None, :], cell_kind[None, :])
    edge = pl.pallas_call(
        edge_kernel,
        out_shape=jax.ShapeDtypeStruct((8 * blocks + 8, 128), F32),
        in_specs=[VMEM, VMEM],
        out_specs=VMEM,
        compiler_params=params(8),
        name="edges",
    )(got, rate_edge)
    pairs = []
    for s in range(slabs):
        after = (s + 1) % slabs
        rank = 1 - s % 2
        pairs += [(rank * slabs + s, rank * slabs + after), (rank * slabs + after, rank * slabs + s)]
    edge_in = lax.ppermute(edge, ("vel", "space"), pairs)
    hi, lo, weights = pl.pallas_call(
        factor_kernel,
        out_shape=(
            jax.ShapeDtypeStruct((H, K), BF16),
            jax.ShapeDtypeStruct((H, K), BF16),
            jax.ShapeDtypeStruct((8, K), F32),
        ),
        in_specs=[ANY, VMEM, ANY],
        out_specs=(VMEM, VMEM, VMEM),
        scratch_shapes=[pltpu.VMEM((2 * (A + B), K), F32), pltpu.SemaphoreType.DMA],
        compiler_params=params(12),
        name="factors",
    )(jnp.asarray(tables()), mode_weights[None, :], edge)
    back = pl.pallas_call(
        collide_kernel,
        out_shape=jax.ShapeDtypeStruct((blocks, own, nv), F32),
        in_specs=[VMEM] * 6,
        out_specs=VMEM,
        scratch_shapes=[
            pltpu.VMEM((V // 128, wide + 4, 128), F32),
            pltpu.VMEM((V // 128, wide + 4, 128), F32),
            pltpu.VMEM((wide, 128), F32),
            pltpu.VMEM((96, V), BF16),
            pltpu.VMEM((wide + 4, V), F32),
            pltpu.VMEM((96, K), BF16),
            pltpu.VMEM((V // 128, 8, 128), F32),
        ],
        compiler_params=params(24),
        name="collide",
    )(got, edge_in, rate, weights, hi, lo)
    result = lax.all_to_all(back, "vel", 0, 0, tiled=True)
    return pl.pallas_call(
        unflip_kernel,
        out_shape=jax.ShapeDtypeStruct((nv, nx), F32),
        in_specs=[VMEM],
        out_specs=VMEM,
        compiler_params=params(8),
        name="unflip",
    )(result)


def solution(mesh):
    return jax.shard_map(
        shards,
        mesh=mesh,
        in_specs=(P("vel", "space"), P("space"), P(), P()),
        out_specs=P("vel", "space"),
        check_vma=False,
    )
```

```python
import functools
import math

import jax
import jax.numpy as jnp
import numpy as np
from jax import lax
from jax.experimental import pallas as pl
from jax.experimental.pallas import tpu as pltpu
from jax.sharding import PartitionSpec as P

V = 4096
K = 512
H = V // 2
B = 64
A = H // B
courant_limit = 0.9
F32 = jnp.float32
BF16 = jnp.bfloat16


def tables():
    k = np.concatenate([np.arange(0, K, 2), np.arange(1, K, 2)])
    scale = np.where(k == 0, math.sqrt(1.0 / V), math.sqrt(2.0 / V))
    fine = (2 * np.arange(B) + 1)[:, None] * k[None, :] % (4 * V) * (math.pi / (2 * V))
    coarse = (2 * B * np.arange(A))[:, None] * k[None, :] % (4 * V) * (math.pi / (2 * V))
    parts = (np.cos(fine) * scale, np.sin(fine) * scale, np.cos(coarse), np.sin(coarse))
    return np.concatenate(parts).astype(np.float32)


def split(x):
    hi = x.astype(BF16)
    return hi, (x - hi.astype(F32)).astype(BF16)


def dot(a, b):
    return lax.dot_general(a, b, (((1,), (0,)), ((), ())), preferred_element_type=F32)


def dot_t(a, b):
    return lax.dot_general(a, b, (((1,), (1,)), ((), ())), preferred_element_type=F32)


def exact_dot(x, picks):
    hi = x.astype(BF16)
    rest = x - hi.astype(F32)
    mid = rest.astype(BF16)
    low = (rest - mid.astype(F32)).astype(BF16)
    return dot(hi, picks) + (dot(mid, picks) + dot(low, picks))


def minmod(a, b):
    return jnp.maximum(jnp.minimum(a, b), jnp.minimum(jnp.maximum(a, b), 0.0))


def upwind(far, near, here, other, speed):
    first = near - far
    second = here - near
    change = minmod(second, other - here) - minmod(first, second)
    return here - speed * (second + 0.5 * (1.0 - speed) * change)


def advect(at, speed, positive):
    if positive:
        return upwind(at(-2), at(-1), at(0), at(1), speed)
    return upwind(at(2), at(1), at(0), at(-1), speed)


def courant_row(velocity):
    return (2 * velocity + 1 - V).astype(F32) * (courant_limit / V)


def mirrored(x):
    lane = lax.broadcasted_iota(jnp.int32, x.shape, 1)
    return jnp.take_along_axis(x, 127 - lane, axis=1)


def place(blocks):
    me = lax.axis_index("vel")
    odd = lax.rem(lax.axis_index("space"), 2)
    return jnp.where(me > 1, me - 1, jnp.where(me == odd, 0, blocks - 1))


def flip_kernel(blocks, f_hbm, out_hbm, f_ref, ext, out_ref, sems, out_sems):
    me = lax.axis_index("vel")
    odd = lax.rem(lax.axis_index("space"), 2)
    nv, nx = f_ref.shape
    own = nx // blocks
    wide = own + 4
    parts = nx // 128
    copies = [
        pltpu.make_async_copy(
            f_hbm.at[:, p * 128 : (p + 1) * 128], f_ref.at[:, p * 128 : (p + 1) * 128], sems.at[p]
        )
        for p in range(parts)
    ]
    for copy in copies:
        copy.start()
    lane = lax.broadcasted_iota(jnp.int32, (1, 128), 1)
    ahead = me >= blocks // 2
    speeds = [jnp.abs(courant_row(me * nv + h * 128 + lane)) for h in range(nv // 128)]

    def rank_of(p):
        return odd if p == 0 else 1 - odd if p == blocks - 1 else p + 1

    def make(p, positive):
        r = rank_of(p)
        for h in range(nv // 128):
            base = 8 + p * own - 2
            out_ref[r, h * wide : (h + 1) * wide, :] = advect(
                lambda k: ext[h, base + k : base + k + wide, :], speeds[h], positive
            )
            if p == 0:
                out_ref[r, h * wide : h * wide + 4, :] = ext[h, 8:12, :]
            if p == blocks - 1:
                out_ref[r, h * wide + own : (h + 1) * wide, :] = ext[h, nx + 4 : nx + 8, :]

    def send(p):
        r = rank_of(p)
        return pltpu.make_async_copy(out_ref.at[r], out_hbm.at[r], out_sems.at[p])

    done = 0
    for p in range(parts):
        copies[p].wait()
        for h in range(nv // 128):
            ext[h, 8 + p * 128 : 8 + (p + 1) * 128, :] = f_ref[
                h * 128 : (h + 1) * 128, p * 128 : (p + 1) * 128
            ].T
        ready = blocks if p == parts - 1 else ((p + 1) * 128 - 4) // own
        for positive in (False, True):

            @pl.when(ahead == positive)
            def _(begin=done, positive=positive, ready=ready):
                for window in range(begin, ready):
                    make(window, positive)

        for window in range(done, ready):
            send(window).start()
        done = ready
    for window in range(blocks):
        send(window).wait()


def rate_kernel(blocks, rates_ref, kind_ref, rate_ref, edge_ref, ext):
    nx = kind_ref.shape[1]
    own = nx // blocks
    kinds = kind_ref[...]
    rate = jnp.zeros(kinds.shape, F32)
    for j in range(rates_ref.shape[1]):
        rate = jnp.where(kinds == j, rates_ref[0, j], rate)
    ext[0:8, :] = jnp.zeros((8, 128), F32)
    ext[8 : nx + 8, :] = jnp.broadcast_to(rate, (128, nx)).T
    ext[nx + 8 :, :] = jnp.zeros((8, 128), F32)
    spot = place(blocks)
    rate_ref[...] = ext[pl.ds(pl.multiple_of(spot * own, own), own + 16), :][6 : own + 10]
    edge_ref[...] = jnp.where(spot == 0, ext[8:16, :], ext[nx + 4 : nx + 12, :])


def edge_kernel(g_ref, rate_ref, out_ref):
    blocks, rows, _ = g_ref.shape
    wide = rows // 2
    first = place(blocks) == 0
    for i in range(blocks):
        for h in range(2):
            n = 8 * i + 4 * h
            out_ref[n : n + 4, :] = jnp.where(
                first,
                g_ref[i, h * wide : h * wide + 4, :],
                g_ref[i, (h + 1) * wide - 4 : (h + 1) * wide, :],
            )
    out_ref[8 * blocks :, :] = rate_ref[...]


def factor_kernel(table_hbm, w_ref, edge_hbm, hi_ref, lo_ref, wp_ref, table, sem):
    copy = pltpu.make_async_copy(table_hbm, table, sem)
    copy.start()
    source = lax.broadcasted_iota(jnp.int32, (K, K), 0)
    target = lax.broadcasted_iota(jnp.int32, (K, K), 1)
    mode = jnp.where(target < K // 2, 2 * target, 2 * target + 1 - K)
    picks = jnp.where(source == mode, 1.0, 0.0).astype(BF16)
    wp_ref[...] = exact_dot(jnp.broadcast_to(w_ref[...], (8, K)), picks)
    copy.wait()

    def body(a, carry):
        f = table[0:B, :] * table[pl.ds(2 * B + a, 1), :] - table[B : 2 * B, :] * table[pl.ds(2 * B + A + a, 1), :]
        hi, lo = split(f)
        rows = pl.ds(pl.multiple_of(a * B, B), B)
        hi_ref[rows, :] = hi
        lo_ref[rows, :] = lo
        return carry

    lax.fori_loop(0, A, body, 0)


def collide_kernel(g_ref, e_ref, rate_in, wp_ref, hi_ref, lo_ref, out_ref, a_ref, b_ref, r_ref, l_ref, c_ref, m_ref, s_ref):
    blocks, rows, _ = g_ref.shape
    wide = rows // 2
    own = wide - 4
    pad = 48
    half = K // 2
    chunks = H // 128
    lane = lax.broadcasted_iota(jnp.int32, (1, 128), 1)
    spot = place(blocks)
    r_ref[...] = rate_in[...]

    def given(n):
        return g_ref[n // 2, (n % 2) * wide : (n % 2 + 1) * wide, :]

    for n in range(2 * chunks):
        b_ref[n, 0:wide, :] = given(n)

    def outer(first):
        for n in range(2 * chunks):
            mine = b_ref[n, 0:4, :] if first else b_ref[n, own:wide, :]
            other = e_ref[4 * n : 4 * n + 4, :]
            s_ref[n, 0:4, :] = other if first else mine
            s_ref[n, 4:8, :] = mine if first else other
            speed = jnp.abs(courant_row(lane + n * 128))
            new = advect(lambda k: s_ref[n, 2 + k : 6 + k, :], speed, n >= chunks)
            if first:
                b_ref[n, 0:4, :] = new
            else:
                b_ref[n, own:wide, :] = new
        if first:
            r_ref[0:2, :] = e_ref[8 * blocks + 2 : 8 * blocks + 4, :]
        else:
            r_ref[own + 2 : wide, :] = e_ref[8 * blocks : 8 * blocks + 2, :]

    @pl.when(spot == 0)
    def _():
        outer(True)

    @pl.when(spot == blocks - 1)
    def _():
        outer(False)

    def fold(c, up, down, at):
        count = up.shape[0]
        for part, first in ((up + down, c * 128), (up - down, H + c * 128)):
            hi, lo = split(part)
            l_ref[0:count, first : first + 128] = hi
            l_ref[at : at + count, first : first + 128] = lo

    def correction(count, at):
        for s in range(2):
            modes = slice(s * half, (s + 1) * half)
            left = l_ref[: 2 * at, s * H : (s + 1) * H]
            both = dot(left, hi_ref[:, modes])
            coef = both[:count] + both[at : at + count] + dot(left[:at], lo_ref[:, modes])[:count]
            hi, lo = split(coef * wp_ref[0:1, modes])
            m_ref[0:count, modes] = hi
            m_ref[at : at + count, modes] = lo
            right = m_ref[: 2 * at, modes]
            back = dot_t(right, hi_ref[:, modes])
            c_ref[:count, s * H : (s + 1) * H] = (
                back[:count] + back[at : at + count] + dot_t(right[:at], lo_ref[:, modes])[:count]
            )

    def corrections(count, c):
        even = c_ref[:count, c * 128 : (c + 1) * 128]
        odd = c_ref[:count, H + c * 128 : H + (c + 1) * 128]
        return even + odd, even - odd

    for c in range(chunks):
        down = mirrored(b_ref[2 * chunks - 1 - c, 0:wide, :])
        a_ref[chunks + c, 0:wide, :] = down
        fold(c, b_ref[c, 0:wide, :], down, pad)
    correction(wide, pad)
    rate = r_ref[...]
    for c in range(chunks):
        plus, minus = corrections(wide, c)
        a_ref[c, 0:wide, :] = b_ref[c, 0:wide, :] - rate * plus
        a_ref[chunks + c, 0:wide, :] = a_ref[chunks + c, 0:wide, :] - rate * minus
        speed = jnp.abs(courant_row(lane + c * 128))
        up = advect(lambda k: a_ref[c, 2 + k : 2 + k + own, :], speed, False)
        down = advect(lambda k: a_ref[chunks + c, 2 + k : 2 + k + own, :], speed, True)
        b_ref[c, 0:own, :] = up
        b_ref[chunks + c, 0:own, :] = down
        fold(c, up, down, own)
    correction(own, own)
    rate = r_ref[2 : own + 2, :]
    for c in range(chunks):
        plus, minus = corrections(own, c)
        n = 2 * chunks - 1 - c
        out_ref[c // 2, :, (c % 2) * 128 : (c % 2 + 1) * 128] = b_ref[c, 0:own, :] - rate * plus
        out_ref[n // 2, :, (n % 2) * 128 : (n % 2 + 1) * 128] = mirrored(
            b_ref[chunks + c, 0:own, :] - rate * minus
        )


def unflip_kernel(t_ref, out_hbm, out_ref, sems):
    blocks, own, _ = t_ref.shape
    odd = lax.rem(lax.axis_index("space"), 2)
    order = [odd] + [p + 1 for p in range(1, blocks - 1)] + [1 - odd]
    per = 128 // own
    copies = []
    for p in range(blocks // per):
        columns = slice(p * 128, (p + 1) * 128)
        rows = jnp.concatenate([t_ref[r] for r in order[p * per : (p + 1) * per]], axis=0)
        out_ref[:, columns] = rows.T
        copies.append(pltpu.make_async_copy(out_ref.at[:, columns], out_hbm.at[:, columns], sems.at[p]))
        copies[-1].start()
    for copy in copies:
        copy.wait()


def params(mib):
    return pltpu.CompilerParams(vmem_limit_bytes=mib * 1024 * 1024)


VMEM = pl.BlockSpec(memory_space=pltpu.VMEM)
SMEM = pl.BlockSpec(memory_space=pltpu.SMEM)
ANY = pl.BlockSpec(memory_space=pl.ANY)


def shards(distribution, cell_kind, type_rates, mode_weights):
    nv, nx = distribution.shape
    blocks = lax.axis_size("vel")
    slabs = lax.axis_size("space")
    own = nx // blocks
    wide = own + 4
    sent = pl.pallas_call(
        functools.partial(flip_kernel, blocks),
        out_shape=jax.ShapeDtypeStruct((blocks, nv // 128 * wide, 128), F32),
        in_specs=[ANY],
        out_specs=ANY,
        scratch_shapes=[
            pltpu.VMEM((nv, nx), F32),
            pltpu.VMEM((nv // 128, nx + 16, 128), F32),
            pltpu.VMEM((blocks, nv // 128 * wide, 128), F32),
            pltpu.SemaphoreType.DMA((nx // 128,)),
            pltpu.SemaphoreType.DMA((blocks,)),
        ],
        compiler_params=params(8),
        name="flip",
    )(pltpu.with_memory_space_constraint(distribution, pltpu.MemorySpace.HBM))
    got = lax.all_to_all(sent, "vel", 0, 0, tiled=True)
    rate, rate_edge = pl.pallas_call(
        functools.partial(rate_kernel, blocks),
        out_shape=(
            jax.ShapeDtypeStruct((wide, 128), F32),
            jax.ShapeDtypeStruct((8, 128), F32),
        ),
        in_specs=[SMEM, VMEM],
        out_specs=(VMEM, VMEM),
        scratch_shapes=[pltpu.VMEM((nx + 16, 128), F32)],
        compiler_params=params(8),
        name="rates",
    )(type_rates[None, :], cell_kind[None, :])
    edge = pl.pallas_call(
        edge_kernel,
        out_shape=jax.ShapeDtypeStruct((8 * blocks + 8, 128), F32),
        in_specs=[VMEM, VMEM],
        out_specs=VMEM,
        compiler_params=params(8),
        name="edges",
    )(got, rate_edge)
    pairs = []
    for s in range(slabs):
        after = (s + 1) % slabs
        rank = 1 - s % 2
        pairs += [(rank * slabs + s, rank * slabs + after), (rank * slabs + after, rank * slabs + s)]
    edge_in = lax.ppermute(edge, ("vel", "space"), pairs)
    hi, lo, weights = pl.pallas_call(
        factor_kernel,
        out_shape=(
            jax.ShapeDtypeStruct((H, K), BF16),
            jax.ShapeDtypeStruct((H, K), BF16),
            jax.ShapeDtypeStruct((8, K), F32),
        ),
        in_specs=[ANY, VMEM, ANY],
        out_specs=(VMEM, VMEM, VMEM),
        scratch_shapes=[pltpu.VMEM((2 * (A + B), K), F32), pltpu.SemaphoreType.DMA],
        compiler_params=params(12),
        name="factors",
    )(jnp.asarray(tables()), mode_weights[None, :], edge)
    back = pl.pallas_call(
        collide_kernel,
        out_shape=jax.ShapeDtypeStruct((blocks, own, nv), F32),
        in_specs=[VMEM] * 6,
        out_specs=VMEM,
        scratch_shapes=[
            pltpu.VMEM((V // 128, wide + 4, 128), F32),
            pltpu.VMEM((V // 128, wide + 4, 128), F32),
            pltpu.VMEM((wide, 128), F32),
            pltpu.VMEM((96, V), BF16),
            pltpu.VMEM((wide + 4, V), F32),
            pltpu.VMEM((96, K), BF16),
            pltpu.VMEM((V // 128, 8, 128), F32),
        ],
        compiler_params=params(24),
        name="collide",
    )(got, edge_in, rate, weights, hi, lo)
    result = lax.all_to_all(back, "vel", 0, 0, tiled=True)
    return pl.pallas_call(
        unflip_kernel,
        out_shape=jax.ShapeDtypeStruct((nv, nx), F32),
        in_specs=[VMEM],
        out_specs=ANY,
        scratch_shapes=[pltpu.VMEM((nv, nx), F32), pltpu.SemaphoreType.DMA((nx // 128,))],
        compiler_params=params(8),
        name="unflip",
    )(result)


def solution(mesh):
    return jax.shard_map(
        shards,
        mesh=mesh,
        in_specs=(P("vel", "space"), P("space"), P(), P()),
        out_specs=P("vel", "space"),
        check_vma=False,
    )
```

```python
import functools
import math

import jax
import jax.numpy as jnp
import numpy as np
from jax import lax
from jax.experimental import pallas as pl
from jax.experimental.pallas import tpu as pltpu
from jax.sharding import PartitionSpec as P

V = 4096
K = 512
H = V // 2
B = 64
A = H // B
courant_limit = 0.9
F32 = jnp.float32
BF16 = jnp.bfloat16


def tables():
    k = np.concatenate([np.arange(0, K, 2), np.arange(1, K, 2)])
    scale = np.where(k == 0, math.sqrt(1.0 / V), math.sqrt(2.0 / V))
    fine = (2 * np.arange(B) + 1)[:, None] * k[None, :] % (4 * V) * (math.pi / (2 * V))
    coarse = (2 * B * np.arange(A))[:, None] * k[None, :] % (4 * V) * (math.pi / (2 * V))
    parts = (np.cos(fine) * scale, np.sin(fine) * scale, np.cos(coarse), np.sin(coarse))
    return np.concatenate(parts).astype(np.float32)


D = 16


def mode_tables():
    v = 2 * np.arange(H) + 1
    rows = []
    for modes in (2 * np.arange(D), 2 * np.arange(D) + 1, 2 * D * np.arange(K // (2 * D))):
        angle = modes[:, None] * v[None, :] % (4 * V) * (math.pi / (2 * V))
        scale = math.sqrt(2.0 / V) if len(rows) < 4 else 1.0
        rows += [np.cos(angle) * scale, np.sin(angle) * scale]
    return np.concatenate(rows).astype(np.float32)


def split(x):
    hi = x.astype(BF16)
    return hi, (x - hi.astype(F32)).astype(BF16)


def dot(a, b):
    return lax.dot_general(a, b, (((1,), (0,)), ((), ())), preferred_element_type=F32)


def exact_dot(x, picks):
    hi = x.astype(BF16)
    rest = x - hi.astype(F32)
    mid = rest.astype(BF16)
    low = (rest - mid.astype(F32)).astype(BF16)
    return dot(hi, picks) + (dot(mid, picks) + dot(low, picks))


def minmod(a, b):
    return jnp.maximum(jnp.minimum(a, b), jnp.minimum(jnp.maximum(a, b), 0.0))


def upwind(far, near, here, other, speed):
    first = near - far
    second = here - near
    change = minmod(second, other - here) - minmod(first, second)
    return here - speed * (second + 0.5 * (1.0 - speed) * change)


def advect(at, speed, positive):
    if positive:
        return upwind(at(-2), at(-1), at(0), at(1), speed)
    return upwind(at(2), at(1), at(0), at(-1), speed)


def courant_row(velocity):
    return (2 * velocity + 1 - V).astype(F32) * (courant_limit / V)


def mirrored(x):
    lane = lax.broadcasted_iota(jnp.int32, x.shape, 1)
    return jnp.take_along_axis(x, 127 - lane, axis=1)


def place(blocks):
    me = lax.axis_index("vel")
    odd = lax.rem(lax.axis_index("space"), 2)
    return jnp.where(me > 1, me - 1, jnp.where(me == odd, 0, blocks - 1))


def flip_kernel(blocks, f_hbm, out_hbm, f_ref, ext, out_ref, sems, out_sems):
    me = lax.axis_index("vel")
    odd = lax.rem(lax.axis_index("space"), 2)
    nv, nx = f_ref.shape
    own = nx // blocks
    wide = own + 4
    parts = nx // 128
    copies = [
        pltpu.make_async_copy(
            f_hbm.at[:, p * 128 : (p + 1) * 128], f_ref.at[:, p * 128 : (p + 1) * 128], sems.at[p]
        )
        for p in range(parts)
    ]
    for copy in copies:
        copy.start()
    lane = lax.broadcasted_iota(jnp.int32, (1, 128), 1)
    ahead = me >= blocks // 2
    speeds = [jnp.abs(courant_row(me * nv + h * 128 + lane)) for h in range(nv // 128)]

    def rank_of(p):
        return odd if p == 0 else 1 - odd if p == blocks - 1 else p + 1

    def make(p, positive):
        r = rank_of(p)
        for h in range(nv // 128):
            base = 8 + p * own - 2
            out_ref[r, h * wide : (h + 1) * wide, :] = advect(
                lambda k: ext[h, base + k : base + k + wide, :], speeds[h], positive
            )
            if p == 0:
                out_ref[r, h * wide : h * wide + 4, :] = ext[h, 8:12, :]
            if p == blocks - 1:
                out_ref[r, h * wide + own : (h + 1) * wide, :] = ext[h, nx + 4 : nx + 8, :]

    def send(p):
        r = rank_of(p)
        return pltpu.make_async_copy(out_ref.at[r], out_hbm.at[r], out_sems.at[p])

    done = 0
    for p in range(parts):
        copies[p].wait()
        for h in range(nv // 128):
            ext[h, 8 + p * 128 : 8 + (p + 1) * 128, :] = f_ref[
                h * 128 : (h + 1) * 128, p * 128 : (p + 1) * 128
            ].T
        ready = blocks if p == parts - 1 else ((p + 1) * 128 - 4) // own
        for positive in (False, True):

            @pl.when(ahead == positive)
            def _(begin=done, positive=positive, ready=ready):
                for window in range(begin, ready):
                    make(window, positive)

        for window in range(done, ready):
            send(window).start()
        done = ready
    for window in range(blocks):
        send(window).wait()


def rate_kernel(blocks, rates_ref, kind_ref, rate_ref, edge_ref, ext):
    nx = kind_ref.shape[1]
    own = nx // blocks
    kinds = kind_ref[...]
    rate = jnp.zeros(kinds.shape, F32)
    for j in range(rates_ref.shape[1]):
        rate = jnp.where(kinds == j, rates_ref[0, j], rate)
    ext[0:8, :] = jnp.zeros((8, 128), F32)
    ext[8 : nx + 8, :] = jnp.broadcast_to(rate, (128, nx)).T
    ext[nx + 8 :, :] = jnp.zeros((8, 128), F32)
    spot = place(blocks)
    rate_ref[...] = ext[pl.ds(pl.multiple_of(spot * own, own), own + 16), :][6 : own + 10]
    edge_ref[...] = jnp.where(spot == 0, ext[8:16, :], ext[nx + 4 : nx + 12, :])


def edge_kernel(g_ref, rate_ref, token_ref, out_ref):
    blocks, rows, _ = g_ref.shape
    wide = rows // 2
    first = place(blocks) == 0
    for i in range(blocks):
        for h in range(2):
            n = 8 * i + 4 * h
            out_ref[n : n + 4, :] = jnp.where(
                first,
                g_ref[i, h * wide : h * wide + 4, :],
                g_ref[i, (h + 1) * wide - 4 : (h + 1) * wide, :],
            )
    out_ref[8 * blocks :, :] = rate_ref[...]


def mode_factor_kernel(table_hbm, sent_hbm, hi_hbm, lo_hbm, token_ref, hi_ref, lo_ref, table, sem, sems):
    token_ref[...] = jnp.zeros_like(token_ref)
    copy = pltpu.make_async_copy(table_hbm, table, sem)
    copy.start()
    copy.wait()
    row = lax.broadcasted_iota(jnp.int32, (D, 1), 0)

    def block(s, c, weight):
        near = 2 * D * s
        f = table[near : near + D, :] * table[pl.ds(4 * D + c, 1), :] - table[
            near + D : near + 2 * D, :
        ] * table[pl.ds(4 * D + K // (2 * D) + c, 1), :]
        if weight is not None:
            f = f * weight
        hi, lo = split(f)
        rows = pl.ds(pl.multiple_of(s * (K // 2) + c * D, D), D)
        hi_ref[rows, :] = hi
        lo_ref[rows, :] = lo

    def body(c, carry):
        block(0, c, None)
        block(1, c, None)
        return carry

    lax.fori_loop(0, K // (2 * D), body, 0)
    block(0, 0, jnp.where(row == 0, math.sqrt(0.5), 1.0))
    stores = [
        pltpu.make_async_copy(hi_ref, hi_hbm, sems.at[0]),
        pltpu.make_async_copy(lo_ref, lo_hbm, sems.at[1]),
    ]
    for store in stores:
        store.start()
    for store in stores:
        store.wait()


def factor_kernel(table_hbm, w_ref, edge_hbm, hi_ref, lo_ref, wp_ref, table, sem):
    copy = pltpu.make_async_copy(table_hbm, table, sem)
    copy.start()
    source = lax.broadcasted_iota(jnp.int32, (K, K), 0)
    target = lax.broadcasted_iota(jnp.int32, (K, K), 1)
    mode = jnp.where(target < K // 2, 2 * target, 2 * target + 1 - K)
    picks = jnp.where(source == mode, 1.0, 0.0).astype(BF16)
    wp_ref[...] = exact_dot(jnp.broadcast_to(w_ref[...], (8, K)), picks)
    copy.wait()

    def body(a, carry):
        f = table[0:B, :] * table[pl.ds(2 * B + a, 1), :] - table[B : 2 * B, :] * table[pl.ds(2 * B + A + a, 1), :]
        hi, lo = split(f)
        rows = pl.ds(pl.multiple_of(a * B, B), B)
        hi_ref[rows, :] = hi
        lo_ref[rows, :] = lo
        return carry

    lax.fori_loop(0, A, body, 0)


def collide_kernel(
    g_ref, e_ref, rate_in, hi_ref, lo_ref, wp_ref, thi_hbm, tlo_hbm,
    out_ref, a_ref, b_ref, r_ref, l_ref, c_ref, m_ref, s_ref, thi_ref, tlo_ref, sems,
):
    blocks, rows, _ = g_ref.shape
    wide = rows // 2
    own = wide - 4
    pad = 48
    half = K // 2
    chunks = H // 128
    lane = lax.broadcasted_iota(jnp.int32, (1, 128), 1)
    spot = place(blocks)
    loads = []
    for n in range(4):
        rows = slice(n // 2 * half, (n // 2 + 1) * half)
        source, target = ((thi_hbm, thi_ref), (tlo_hbm, tlo_ref))[n % 2]
        loads.append(pltpu.make_async_copy(source.at[rows, :], target.at[rows, :], sems.at[n]))
        loads[n].start()
    r_ref[...] = rate_in[...]

    def given(n):
        return g_ref[n // 2, (n % 2) * wide : (n % 2 + 1) * wide, :]

    for n in range(2 * chunks):
        b_ref[n, 0:wide, :] = given(n)

    def outer(first):
        for n in range(2 * chunks):
            mine = b_ref[n, 0:4, :] if first else b_ref[n, own:wide, :]
            other = e_ref[4 * n : 4 * n + 4, :]
            s_ref[n, 0:4, :] = other if first else mine
            s_ref[n, 4:8, :] = mine if first else other
            speed = jnp.abs(courant_row(lane + n * 128))
            new = advect(lambda k: s_ref[n, 2 + k : 6 + k, :], speed, n >= chunks)
            if first:
                b_ref[n, 0:4, :] = new
            else:
                b_ref[n, own:wide, :] = new
        if first:
            r_ref[0:2, :] = e_ref[8 * blocks + 2 : 8 * blocks + 4, :]
        else:
            r_ref[own + 2 : wide, :] = e_ref[8 * blocks : 8 * blocks + 2, :]

    @pl.when(spot == 0)
    def _():
        outer(True)

    @pl.when(spot == blocks - 1)
    def _():
        outer(False)

    def fold(c, up, down, at):
        count = up.shape[0]
        for part, first in ((up + down, c * 128), (up - down, H + c * 128)):
            hi, lo = split(part)
            l_ref[0:count, first : first + 128] = hi
            l_ref[at : at + count, first : first + 128] = lo

    def correction(count, at):
        for s in range(2):
            modes = slice(s * half, (s + 1) * half)
            left = l_ref[: 2 * at, s * H : (s + 1) * H]
            both = dot(left, hi_ref[:, modes])
            coef = both[:count] + both[at : at + count] + dot(left[:at], lo_ref[:, modes])[:count]
            hi, lo = split(coef * wp_ref[0:1, modes])
            m_ref[0:count, modes] = hi
            m_ref[at : at + count, modes] = lo
            right = m_ref[: 2 * at, modes]
            if count == wide:
                loads[2 * s].wait()
                loads[2 * s + 1].wait()
            back = dot(right, thi_ref[modes, :])
            c_ref[:count, s * H : (s + 1) * H] = (
                back[:count] + back[at : at + count] + dot(right[:at], tlo_ref[modes, :])[:count]
            )

    def corrections(count, c):
        even = c_ref[:count, c * 128 : (c + 1) * 128]
        odd = c_ref[:count, H + c * 128 : H + (c + 1) * 128]
        return even + odd, even - odd

    for c in range(chunks):
        down = mirrored(b_ref[2 * chunks - 1 - c, 0:wide, :])
        a_ref[chunks + c, 0:wide, :] = down
        fold(c, b_ref[c, 0:wide, :], down, pad)
    correction(wide, pad)
    rate = r_ref[...]
    for c in range(chunks):
        plus, minus = corrections(wide, c)
        a_ref[c, 0:wide, :] = b_ref[c, 0:wide, :] - rate * plus
        a_ref[chunks + c, 0:wide, :] = a_ref[chunks + c, 0:wide, :] - rate * minus
        speed = jnp.abs(courant_row(lane + c * 128))
        up = advect(lambda k: a_ref[c, 2 + k : 2 + k + own, :], speed, False)
        down = advect(lambda k: a_ref[chunks + c, 2 + k : 2 + k + own, :], speed, True)
        b_ref[c, 0:own, :] = up
        b_ref[chunks + c, 0:own, :] = down
        fold(c, up, down, own)
    correction(own, own)
    rate = r_ref[2 : own + 2, :]
    for c in range(chunks):
        plus, minus = corrections(own, c)
        n = 2 * chunks - 1 - c
        out_ref[c // 2, :, (c % 2) * 128 : (c % 2 + 1) * 128] = b_ref[c, 0:own, :] - rate * plus
        out_ref[n // 2, :, (n % 2) * 128 : (n % 2 + 1) * 128] = mirrored(
            b_ref[chunks + c, 0:own, :] - rate * minus
        )


def unflip_kernel(t_ref, out_hbm, out_ref, sems):
    blocks, own, _ = t_ref.shape
    odd = lax.rem(lax.axis_index("space"), 2)
    order = [odd] + [p + 1 for p in range(1, blocks - 1)] + [1 - odd]
    per = 128 // own
    copies = []
    for p in range(blocks // per):
        columns = slice(p * 128, (p + 1) * 128)
        rows = jnp.concatenate([t_ref[r] for r in order[p * per : (p + 1) * per]], axis=0)
        out_ref[:, columns] = rows.T
        copies.append(pltpu.make_async_copy(out_ref.at[:, columns], out_hbm.at[:, columns], sems.at[p]))
        copies[-1].start()
    for copy in copies:
        copy.wait()


def params(mib):
    return pltpu.CompilerParams(vmem_limit_bytes=mib * 1024 * 1024)


VMEM = pl.BlockSpec(memory_space=pltpu.VMEM)
SMEM = pl.BlockSpec(memory_space=pltpu.SMEM)
ANY = pl.BlockSpec(memory_space=pl.ANY)


def shards(distribution, cell_kind, type_rates, mode_weights):
    nv, nx = distribution.shape
    blocks = lax.axis_size("vel")
    slabs = lax.axis_size("space")
    own = nx // blocks
    wide = own + 4
    sent = pl.pallas_call(
        functools.partial(flip_kernel, blocks),
        out_shape=jax.ShapeDtypeStruct((blocks, nv // 128 * wide, 128), F32),
        in_specs=[ANY],
        out_specs=ANY,
        scratch_shapes=[
            pltpu.VMEM((nv, nx), F32),
            pltpu.VMEM((nv // 128, nx + 16, 128), F32),
            pltpu.VMEM((blocks, nv // 128 * wide, 128), F32),
            pltpu.SemaphoreType.DMA((nx // 128,)),
            pltpu.SemaphoreType.DMA((blocks,)),
        ],
        compiler_params=params(8),
        name="flip",
    )(pltpu.with_memory_space_constraint(distribution, pltpu.MemorySpace.HBM))
    got = lax.all_to_all(sent, "vel", 0, 0, tiled=True)
    rate, rate_edge = pl.pallas_call(
        functools.partial(rate_kernel, blocks),
        out_shape=(
            jax.ShapeDtypeStruct((wide, 128), F32),
            jax.ShapeDtypeStruct((8, 128), F32),
        ),
        in_specs=[SMEM, VMEM],
        out_specs=(VMEM, VMEM),
        scratch_shapes=[pltpu.VMEM((nx + 16, 128), F32)],
        compiler_params=params(8),
        name="rates",
    )(type_rates[None, :], cell_kind[None, :])
    *by_modes, token = pl.pallas_call(
        mode_factor_kernel,
        out_shape=(
            pltpu.MemorySpace.HBM((K, H), BF16),
            pltpu.MemorySpace.HBM((K, H), BF16),
            jax.ShapeDtypeStruct((8, 128), F32),
        ),
        in_specs=[ANY, ANY],
        out_specs=(ANY, ANY, VMEM),
        scratch_shapes=[
            pltpu.VMEM((K, H), BF16),
            pltpu.VMEM((K, H), BF16),
            pltpu.VMEM((4 * D + K // D, H), F32),
            pltpu.SemaphoreType.DMA,
            pltpu.SemaphoreType.DMA((2,)),
        ],
        compiler_params=params(16),
        name="mode_factors",
    )(jnp.asarray(mode_tables()), sent)
    edge = pl.pallas_call(
        edge_kernel,
        out_shape=jax.ShapeDtypeStruct((8 * blocks + 8, 128), F32),
        in_specs=[VMEM, VMEM, VMEM],
        out_specs=VMEM,
        compiler_params=params(8),
        name="edges",
    )(got, rate_edge, token)
    pairs = []
    for s in range(slabs):
        after = (s + 1) % slabs
        rank = 1 - s % 2
        pairs += [(rank * slabs + s, rank * slabs + after), (rank * slabs + after, rank * slabs + s)]
    edge_in = lax.ppermute(edge, ("vel", "space"), pairs)
    by_modes = [pltpu.with_memory_space_constraint(part, pltpu.MemorySpace.HBM) for part in by_modes]
    factors = pl.pallas_call(
        factor_kernel,
        out_shape=(
            jax.ShapeDtypeStruct((H, K), BF16),
            jax.ShapeDtypeStruct((H, K), BF16),
            jax.ShapeDtypeStruct((8, K), F32),
        ),
        in_specs=[ANY, VMEM, ANY],
        out_specs=(VMEM,) * 3,
        scratch_shapes=[pltpu.VMEM((2 * (A + B), K), F32), pltpu.SemaphoreType.DMA],
        compiler_params=params(12),
        name="factors",
    )(jnp.asarray(tables()), mode_weights[None, :], edge)
    back = pl.pallas_call(
        collide_kernel,
        out_shape=jax.ShapeDtypeStruct((blocks, own, nv), F32),
        in_specs=[VMEM] * 6 + [ANY] * 2,
        out_specs=VMEM,
        scratch_shapes=[
            pltpu.VMEM((V // 128, wide + 4, 128), F32),
            pltpu.VMEM((V // 128, wide + 4, 128), F32),
            pltpu.VMEM((wide, 128), F32),
            pltpu.VMEM((96, V), BF16),
            pltpu.VMEM((wide + 4, V), F32),
            pltpu.VMEM((96, K), BF16),
            pltpu.VMEM((V // 128, 8, 128), F32),
            pltpu.VMEM((K, H), BF16),
            pltpu.VMEM((K, H), BF16),
            pltpu.SemaphoreType.DMA((4,)),
        ],
        compiler_params=params(24),
        name="collide",
    )(got, edge_in, rate, *factors, *by_modes)
    result = lax.all_to_all(back, "vel", 0, 0, tiled=True)
    return pl.pallas_call(
        unflip_kernel,
        out_shape=jax.ShapeDtypeStruct((nv, nx), F32),
        in_specs=[VMEM],
        out_specs=ANY,
        scratch_shapes=[pltpu.VMEM((nv, nx), F32), pltpu.SemaphoreType.DMA((nx // 128,))],
        compiler_params=params(8),
        name="unflip",
    )(result)


def solution(mesh):
    return jax.shard_map(
        shards,
        mesh=mesh,
        in_specs=(P("vel", "space"), P("space"), P(), P()),
        out_specs=P("vel", "space"),
        check_vma=False,
    )
```

```python
import functools
import math

import jax
import jax.numpy as jnp
import numpy as np
from jax import lax
from jax.experimental import pallas as pl
from jax.experimental.pallas import tpu as pltpu
from jax.sharding import PartitionSpec as P

V = 4096
K = 512
H = V // 2
B = 64
A = H // B
courant_limit = 0.9
F32 = jnp.float32
BF16 = jnp.bfloat16


def tables():
    k = np.concatenate([np.arange(0, K, 2), np.arange(1, K, 2)])
    scale = np.where(k == 0, math.sqrt(1.0 / V), math.sqrt(2.0 / V))
    fine = (2 * np.arange(B) + 1)[:, None] * k[None, :] % (4 * V) * (math.pi / (2 * V))
    coarse = (2 * B * np.arange(A))[:, None] * k[None, :] % (4 * V) * (math.pi / (2 * V))
    parts = (np.cos(fine) * scale, np.sin(fine) * scale, np.cos(coarse), np.sin(coarse))
    return np.concatenate(parts).astype(np.float32)


D = 16


def mode_tables():
    v = 2 * np.arange(H) + 1
    rows = []
    for modes in (2 * np.arange(D), 2 * np.arange(D) + 1, 2 * D * np.arange(K // (2 * D))):
        angle = modes[:, None] * v[None, :] % (4 * V) * (math.pi / (2 * V))
        scale = math.sqrt(2.0 / V) if len(rows) < 4 else 1.0
        rows += [np.cos(angle) * scale, np.sin(angle) * scale]
    return np.concatenate(rows).astype(np.float32)


def split(x):
    hi = x.astype(BF16)
    return hi, (x - hi.astype(F32)).astype(BF16)


def dot(a, b):
    return lax.dot_general(a, b, (((1,), (0,)), ((), ())), preferred_element_type=F32)


def exact_dot(x, picks):
    hi = x.astype(BF16)
    rest = x - hi.astype(F32)
    mid = rest.astype(BF16)
    low = (rest - mid.astype(F32)).astype(BF16)
    return dot(hi, picks) + (dot(mid, picks) + dot(low, picks))


def minmod(a, b):
    return jnp.maximum(jnp.minimum(a, b), jnp.minimum(jnp.maximum(a, b), 0.0))


def upwind(far, near, here, other, speed):
    first = near - far
    second = here - near
    change = minmod(second, other - here) - minmod(first, second)
    return here - speed * (second + 0.5 * (1.0 - speed) * change)


def advect(at, speed, positive):
    if positive:
        return upwind(at(-2), at(-1), at(0), at(1), speed)
    return upwind(at(2), at(1), at(0), at(-1), speed)


def courant_row(velocity):
    return (2 * velocity + 1 - V).astype(F32) * (courant_limit / V)


def mirrored(x):
    lane = lax.broadcasted_iota(jnp.int32, x.shape, 1)
    return jnp.take_along_axis(x, 127 - lane, axis=1)


def place(blocks):
    me = lax.axis_index("vel")
    odd = lax.rem(lax.axis_index("space"), 2)
    return jnp.where(me > 1, me - 1, jnp.where(me == odd, 0, blocks - 1))


def flip_kernel(blocks, f_hbm, out_hbm, f_ref, ext, out_ref, sems, out_sems):
    me = lax.axis_index("vel")
    odd = lax.rem(lax.axis_index("space"), 2)
    nv, nx = f_ref.shape
    own = nx // blocks
    wide = own + 4
    parts = nx // 128
    copies = [
        pltpu.make_async_copy(
            f_hbm.at[:, p * 128 : (p + 1) * 128], f_ref.at[:, p * 128 : (p + 1) * 128], sems.at[p]
        )
        for p in range(parts)
    ]
    for copy in copies:
        copy.start()
    lane = lax.broadcasted_iota(jnp.int32, (1, 128), 1)
    ahead = me >= blocks // 2
    speeds = [jnp.abs(courant_row(me * nv + h * 128 + lane)) for h in range(nv // 128)]

    def rank_of(p):
        return odd if p == 0 else 1 - odd if p == blocks - 1 else p + 1

    def make(p, positive):
        r = rank_of(p)
        for h in range(nv // 128):
            base = 8 + p * own - 2
            out_ref[r, h * wide : (h + 1) * wide, :] = advect(
                lambda k: ext[h, base + k : base + k + wide, :], speeds[h], positive
            )
            if p == 0:
                out_ref[r, h * wide : h * wide + 4, :] = ext[h, 8:12, :]
            if p == blocks - 1:
                out_ref[r, h * wide + own : (h + 1) * wide, :] = ext[h, nx + 4 : nx + 8, :]

    def send(p):
        r = rank_of(p)
        return pltpu.make_async_copy(out_ref.at[r], out_hbm.at[r], out_sems.at[p])

    done = 0
    for p in range(parts):
        copies[p].wait()
        for h in range(nv // 128):
            ext[h, 8 + p * 128 : 8 + (p + 1) * 128, :] = f_ref[
                h * 128 : (h + 1) * 128, p * 128 : (p + 1) * 128
            ].T
        ready = blocks if p == parts - 1 else ((p + 1) * 128 - 4) // own
        for positive in (False, True):

            @pl.when(ahead == positive)
            def _(begin=done, positive=positive, ready=ready):
                for window in range(begin, ready):
                    make(window, positive)

        for window in range(done, ready):
            send(window).start()
        done = ready
    for window in range(blocks):
        send(window).wait()


def rate_kernel(blocks, rates_ref, kind_ref, rate_ref, edge_ref, ext):
    nx = kind_ref.shape[1]
    own = nx // blocks
    kinds = kind_ref[...]
    rate = jnp.zeros(kinds.shape, F32)
    for j in range(rates_ref.shape[1]):
        rate = jnp.where(kinds == j, rates_ref[0, j], rate)
    ext[0:8, :] = jnp.zeros((8, 128), F32)
    ext[8 : nx + 8, :] = jnp.broadcast_to(rate, (128, nx)).T
    ext[nx + 8 :, :] = jnp.zeros((8, 128), F32)
    spot = place(blocks)
    rate_ref[...] = ext[pl.ds(pl.multiple_of(spot * own, own), own + 16), :][6 : own + 10]
    edge_ref[...] = jnp.where(spot == 0, ext[8:16, :], ext[nx + 4 : nx + 12, :])


def edge_kernel(g_ref, rate_ref, token_ref, out_ref):
    blocks, rows, _ = g_ref.shape
    wide = rows // 2
    first = place(blocks) == 0
    for i in range(blocks):
        for h in range(2):
            n = 8 * i + 4 * h
            out_ref[n : n + 4, :] = jnp.where(
                first,
                g_ref[i, h * wide : h * wide + 4, :],
                g_ref[i, (h + 1) * wide - 4 : (h + 1) * wide, :],
            )
    out_ref[8 * blocks :, :] = rate_ref[...]


def mode_factor_kernel(table_hbm, sent_hbm, hi_hbm, lo_hbm, token_ref, hi_ref, lo_ref, table, sem, sems):
    token_ref[...] = jnp.zeros_like(token_ref)
    copy = pltpu.make_async_copy(table_hbm, table, sem)
    copy.start()
    copy.wait()
    row = lax.broadcasted_iota(jnp.int32, (D, 1), 0)

    def block(s, c, weight):
        near = 2 * D * s
        f = table[near : near + D, :] * table[pl.ds(4 * D + c, 1), :] - table[
            near + D : near + 2 * D, :
        ] * table[pl.ds(4 * D + K // (2 * D) + c, 1), :]
        if weight is not None:
            f = f * weight
        hi, lo = split(f)
        rows = pl.ds(pl.multiple_of(s * (K // 2) + c * D, D), D)
        hi_ref[rows, :] = hi
        lo_ref[rows, :] = lo

    def body(c, carry):
        block(0, c, None)
        block(1, c, None)
        return carry

    lax.fori_loop(0, K // (2 * D), body, 0)
    block(0, 0, jnp.where(row == 0, math.sqrt(0.5), 1.0))
    stores = [
        pltpu.make_async_copy(hi_ref, hi_hbm, sems.at[0]),
        pltpu.make_async_copy(lo_ref, lo_hbm, sems.at[1]),
    ]
    for store in stores:
        store.start()
    for store in stores:
        store.wait()


def factor_kernel(table_hbm, w_ref, edge_hbm, thi_hbm, hi_ref, lo_ref, wp_ref, thi_ref, table, sem, load_sem):
    copy = pltpu.make_async_copy(table_hbm, table, sem)
    copy.start()
    load = pltpu.make_async_copy(thi_hbm, thi_ref, load_sem)
    load.start()
    source = lax.broadcasted_iota(jnp.int32, (K, K), 0)
    target = lax.broadcasted_iota(jnp.int32, (K, K), 1)
    mode = jnp.where(target < K // 2, 2 * target, 2 * target + 1 - K)
    picks = jnp.where(source == mode, 1.0, 0.0).astype(BF16)
    wp_ref[...] = exact_dot(jnp.broadcast_to(w_ref[...], (8, K)), picks)
    copy.wait()

    def body(a, carry):
        f = table[0:B, :] * table[pl.ds(2 * B + a, 1), :] - table[B : 2 * B, :] * table[pl.ds(2 * B + A + a, 1), :]
        hi, lo = split(f)
        rows = pl.ds(pl.multiple_of(a * B, B), B)
        hi_ref[rows, :] = hi
        lo_ref[rows, :] = lo
        return carry

    lax.fori_loop(0, A, body, 0)
    load.wait()


def collide_kernel(
    g_ref, e_ref, rate_in, hi_ref, lo_ref, wp_ref, thi_ref, tlo_hbm,
    out_ref, a_ref, b_ref, r_ref, l_ref, c_ref, m_ref, s_ref, tlo_ref, sems,
):
    blocks, rows, _ = g_ref.shape
    wide = rows // 2
    own = wide - 4
    pad = 48
    half = K // 2
    chunks = H // 128
    lane = lax.broadcasted_iota(jnp.int32, (1, 128), 1)
    spot = place(blocks)
    loads = []
    for n in range(2):
        rows = slice(n * half, (n + 1) * half)
        loads.append(pltpu.make_async_copy(tlo_hbm.at[rows, :], tlo_ref.at[rows, :], sems.at[n]))
        loads[n].start()
    r_ref[...] = rate_in[...]

    def given(n):
        return g_ref[n // 2, (n % 2) * wide : (n % 2 + 1) * wide, :]

    for n in range(2 * chunks):
        b_ref[n, 0:wide, :] = given(n)

    def outer(first):
        for n in range(2 * chunks):
            mine = b_ref[n, 0:4, :] if first else b_ref[n, own:wide, :]
            other = e_ref[4 * n : 4 * n + 4, :]
            s_ref[n, 0:4, :] = other if first else mine
            s_ref[n, 4:8, :] = mine if first else other
            speed = jnp.abs(courant_row(lane + n * 128))
            new = advect(lambda k: s_ref[n, 2 + k : 6 + k, :], speed, n >= chunks)
            if first:
                b_ref[n, 0:4, :] = new
            else:
                b_ref[n, own:wide, :] = new
        if first:
            r_ref[0:2, :] = e_ref[8 * blocks + 2 : 8 * blocks + 4, :]
        else:
            r_ref[own + 2 : wide, :] = e_ref[8 * blocks : 8 * blocks + 2, :]

    @pl.when(spot == 0)
    def _():
        outer(True)

    @pl.when(spot == blocks - 1)
    def _():
        outer(False)

    def fold(c, up, down, at):
        count = up.shape[0]
        for part, first in ((up + down, c * 128), (up - down, H + c * 128)):
            hi, lo = split(part)
            l_ref[0:count, first : first + 128] = hi
            l_ref[at : at + count, first : first + 128] = lo

    def correction(count, at):
        for s in range(2):
            modes = slice(s * half, (s + 1) * half)
            left = l_ref[: 2 * at, s * H : (s + 1) * H]
            both = dot(left, hi_ref[:, modes])
            coef = both[:count] + both[at : at + count] + dot(left[:at], lo_ref[:, modes])[:count]
            hi, lo = split(coef * wp_ref[0:1, modes])
            m_ref[0:count, modes] = hi
            m_ref[at : at + count, modes] = lo
        for s in range(2):
            modes = slice(s * half, (s + 1) * half)
            right = m_ref[: 2 * at, modes]
            if count == wide:
                loads[s].wait()
            back = dot(right, thi_ref[modes, :])
            c_ref[:count, s * H : (s + 1) * H] = (
                back[:count] + back[at : at + count] + dot(right[:at], tlo_ref[modes, :])[:count]
            )

    def corrections(count, c):
        even = c_ref[:count, c * 128 : (c + 1) * 128]
        odd = c_ref[:count, H + c * 128 : H + (c + 1) * 128]
        return even + odd, even - odd

    for c in range(chunks):
        down = mirrored(b_ref[2 * chunks - 1 - c, 0:wide, :])
        a_ref[chunks + c, 0:wide, :] = down
        fold(c, b_ref[c, 0:wide, :], down, pad)
    correction(wide, pad)
    rate = r_ref[...]
    for c in range(chunks):
        plus, minus = corrections(wide, c)
        a_ref[c, 0:wide, :] = b_ref[c, 0:wide, :] - rate * plus
        a_ref[chunks + c, 0:wide, :] = a_ref[chunks + c, 0:wide, :] - rate * minus
        speed = jnp.abs(courant_row(lane + c * 128))
        up = advect(lambda k: a_ref[c, 2 + k : 2 + k + own, :], speed, False)
        down = advect(lambda k: a_ref[chunks + c, 2 + k : 2 + k + own, :], speed, True)
        b_ref[c, 0:own, :] = up
        b_ref[chunks + c, 0:own, :] = down
        fold(c, up, down, own)
    correction(own, own)
    rate = r_ref[2 : own + 2, :]
    for c in range(chunks):
        plus, minus = corrections(own, c)
        n = 2 * chunks - 1 - c
        out_ref[c // 2, :, (c % 2) * 128 : (c % 2 + 1) * 128] = b_ref[c, 0:own, :] - rate * plus
        out_ref[n // 2, :, (n % 2) * 128 : (n % 2 + 1) * 128] = mirrored(
            b_ref[chunks + c, 0:own, :] - rate * minus
        )


def unflip_kernel(t_ref, out_hbm, out_ref, sems):
    blocks, own, _ = t_ref.shape
    odd = lax.rem(lax.axis_index("space"), 2)
    order = [odd] + [p + 1 for p in range(1, blocks - 1)] + [1 - odd]
    per = 128 // own
    copies = []
    for p in range(blocks // per):
        columns = slice(p * 128, (p + 1) * 128)
        rows = jnp.concatenate([t_ref[r] for r in order[p * per : (p + 1) * per]], axis=0)
        out_ref[:, columns] = rows.T
        copies.append(pltpu.make_async_copy(out_ref.at[:, columns], out_hbm.at[:, columns], sems.at[p]))
        copies[-1].start()
    for copy in copies:
        copy.wait()


def params(mib):
    return pltpu.CompilerParams(vmem_limit_bytes=mib * 1024 * 1024)


VMEM = pl.BlockSpec(memory_space=pltpu.VMEM)
SMEM = pl.BlockSpec(memory_space=pltpu.SMEM)
ANY = pl.BlockSpec(memory_space=pl.ANY)


def shards(distribution, cell_kind, type_rates, mode_weights):
    nv, nx = distribution.shape
    blocks = lax.axis_size("vel")
    slabs = lax.axis_size("space")
    own = nx // blocks
    wide = own + 4
    sent = pl.pallas_call(
        functools.partial(flip_kernel, blocks),
        out_shape=jax.ShapeDtypeStruct((blocks, nv // 128 * wide, 128), F32),
        in_specs=[ANY],
        out_specs=ANY,
        scratch_shapes=[
            pltpu.VMEM((nv, nx), F32),
            pltpu.VMEM((nv // 128, nx + 16, 128), F32),
            pltpu.VMEM((blocks, nv // 128 * wide, 128), F32),
            pltpu.SemaphoreType.DMA((nx // 128,)),
            pltpu.SemaphoreType.DMA((blocks,)),
        ],
        compiler_params=params(8),
        name="flip",
    )(pltpu.with_memory_space_constraint(distribution, pltpu.MemorySpace.HBM))
    got = lax.all_to_all(sent, "vel", 0, 0, tiled=True)
    rate, rate_edge = pl.pallas_call(
        functools.partial(rate_kernel, blocks),
        out_shape=(
            jax.ShapeDtypeStruct((wide, 128), F32),
            jax.ShapeDtypeStruct((8, 128), F32),
        ),
        in_specs=[SMEM, VMEM],
        out_specs=(VMEM, VMEM),
        scratch_shapes=[pltpu.VMEM((nx + 16, 128), F32)],
        compiler_params=params(8),
        name="rates",
    )(type_rates[None, :], cell_kind[None, :])
    *by_modes, token = pl.pallas_call(
        mode_factor_kernel,
        out_shape=(
            pltpu.MemorySpace.HBM((K, H), BF16),
            pltpu.MemorySpace.HBM((K, H), BF16),
            jax.ShapeDtypeStruct((8, 128), F32),
        ),
        in_specs=[ANY, ANY],
        out_specs=(ANY, ANY, VMEM),
        scratch_shapes=[
            pltpu.VMEM((K, H), BF16),
            pltpu.VMEM((K, H), BF16),
            pltpu.VMEM((4 * D + K // D, H), F32),
            pltpu.SemaphoreType.DMA,
            pltpu.SemaphoreType.DMA((2,)),
        ],
        compiler_params=params(16),
        name="mode_factors",
    )(jnp.asarray(mode_tables()), sent)
    edge = pl.pallas_call(
        edge_kernel,
        out_shape=jax.ShapeDtypeStruct((8 * blocks + 8, 128), F32),
        in_specs=[VMEM, VMEM, VMEM],
        out_specs=VMEM,
        compiler_params=params(8),
        name="edges",
    )(got, rate_edge, token)
    pairs = []
    for s in range(slabs):
        after = (s + 1) % slabs
        rank = 1 - s % 2
        pairs += [(rank * slabs + s, rank * slabs + after), (rank * slabs + after, rank * slabs + s)]
    edge_in = lax.ppermute(edge, ("vel", "space"), pairs)
    by_modes = [pltpu.with_memory_space_constraint(part, pltpu.MemorySpace.HBM) for part in by_modes]
    factors = pl.pallas_call(
        factor_kernel,
        out_shape=(
            jax.ShapeDtypeStruct((H, K), BF16),
            jax.ShapeDtypeStruct((H, K), BF16),
            jax.ShapeDtypeStruct((8, K), F32),
            jax.ShapeDtypeStruct((K, H), BF16),
        ),
        in_specs=[ANY, VMEM, ANY, ANY],
        out_specs=(VMEM,) * 4,
        scratch_shapes=[
            pltpu.VMEM((2 * (A + B), K), F32),
            pltpu.SemaphoreType.DMA,
            pltpu.SemaphoreType.DMA,
        ],
        compiler_params=params(14),
        name="factors",
    )(jnp.asarray(tables()), mode_weights[None, :], edge, by_modes[0])
    back = pl.pallas_call(
        collide_kernel,
        out_shape=jax.ShapeDtypeStruct((blocks, own, nv), F32),
        in_specs=[VMEM] * 7 + [ANY],
        out_specs=VMEM,
        scratch_shapes=[
            pltpu.VMEM((V // 128, wide + 4, 128), F32),
            pltpu.VMEM((V // 128, wide + 4, 128), F32),
            pltpu.VMEM((wide, 128), F32),
            pltpu.VMEM((96, V), BF16),
            pltpu.VMEM((wide + 4, V), F32),
            pltpu.VMEM((96, K), BF16),
            pltpu.VMEM((V // 128, 8, 128), F32),
            pltpu.VMEM((K, H), BF16),
            pltpu.SemaphoreType.DMA((2,)),
        ],
        compiler_params=params(24),
        name="collide",
    )(got, edge_in, rate, *factors, by_modes[1])
    result = lax.all_to_all(back, "vel", 0, 0, tiled=True)
    return pl.pallas_call(
        unflip_kernel,
        out_shape=jax.ShapeDtypeStruct((nv, nx), F32),
        in_specs=[VMEM],
        out_specs=ANY,
        scratch_shapes=[pltpu.VMEM((nv, nx), F32), pltpu.SemaphoreType.DMA((nx // 128,))],
        compiler_params=params(8),
        name="unflip",
    )(result)


def solution(mesh):
    return jax.shard_map(
        shards,
        mesh=mesh,
        in_specs=(P("vel", "space"), P("space"), P(), P()),
        out_specs=P("vel", "space"),
        check_vma=False,
    )
```

```python
import functools
import math

import jax
import jax.numpy as jnp
import numpy as np
from jax import lax
from jax.experimental import pallas as pl
from jax.experimental.pallas import tpu as pltpu
from jax.sharding import PartitionSpec as P

V = 4096
K = 512
H = V // 2
B = 64
A = H // B
courant_limit = 0.9
F32 = jnp.float32
BF16 = jnp.bfloat16


def tables():
    k = np.concatenate([np.arange(0, K, 2), np.arange(1, K, 2)])
    scale = np.where(k == 0, math.sqrt(1.0 / V), math.sqrt(2.0 / V))
    fine = (2 * np.arange(B) + 1)[:, None] * k[None, :] % (4 * V) * (math.pi / (2 * V))
    coarse = (2 * B * np.arange(A))[:, None] * k[None, :] % (4 * V) * (math.pi / (2 * V))
    parts = (np.cos(fine) * scale, np.sin(fine) * scale, np.cos(coarse), np.sin(coarse))
    return np.concatenate(parts).astype(np.float32)


D = 16


def mode_tables():
    v = 2 * np.arange(H) + 1
    rows = []
    for modes in (2 * np.arange(D), 2 * np.arange(D) + 1, 2 * D * np.arange(K // (2 * D))):
        angle = modes[:, None] * v[None, :] % (4 * V) * (math.pi / (2 * V))
        scale = math.sqrt(2.0 / V) if len(rows) < 4 else 1.0
        rows += [np.cos(angle) * scale, np.sin(angle) * scale]
    return np.concatenate(rows).astype(np.float32)


def split(x):
    hi = x.astype(BF16)
    return hi, (x - hi.astype(F32)).astype(BF16)


def dot(a, b):
    return lax.dot_general(a, b, (((1,), (0,)), ((), ())), preferred_element_type=F32)


def exact_dot(x, picks):
    hi = x.astype(BF16)
    rest = x - hi.astype(F32)
    mid = rest.astype(BF16)
    low = (rest - mid.astype(F32)).astype(BF16)
    return dot(hi, picks) + (dot(mid, picks) + dot(low, picks))


def minmod(a, b):
    return jnp.maximum(jnp.minimum(a, b), jnp.minimum(jnp.maximum(a, b), 0.0))


def upwind(far, near, here, other, speed):
    first = near - far
    second = here - near
    change = minmod(second, other - here) - minmod(first, second)
    return here - speed * (second + 0.5 * (1.0 - speed) * change)


def advect(at, speed, positive):
    if positive:
        return upwind(at(-2), at(-1), at(0), at(1), speed)
    return upwind(at(2), at(1), at(0), at(-1), speed)


def courant_row(velocity):
    return (2 * velocity + 1 - V).astype(F32) * (courant_limit / V)


def mirrored(x):
    lane = lax.broadcasted_iota(jnp.int32, x.shape, 1)
    return jnp.take_along_axis(x, 127 - lane, axis=1)


def place(blocks):
    me = lax.axis_index("vel")
    odd = lax.rem(lax.axis_index("space"), 2)
    return jnp.where(me > 1, me - 1, jnp.where(me == odd, 0, blocks - 1))


def flip_kernel(blocks, f_hbm, out_hbm, f_ref, ext, out_ref, sems, out_sems):
    me = lax.axis_index("vel")
    odd = lax.rem(lax.axis_index("space"), 2)
    nv, nx = f_ref.shape
    own = nx // blocks
    wide = own + 4
    parts = nx // 128
    copies = [
        pltpu.make_async_copy(
            f_hbm.at[:, p * 128 : (p + 1) * 128], f_ref.at[:, p * 128 : (p + 1) * 128], sems.at[p]
        )
        for p in range(parts)
    ]
    for copy in copies:
        copy.start()
    lane = lax.broadcasted_iota(jnp.int32, (1, 128), 1)
    ahead = me >= blocks // 2
    speeds = [jnp.abs(courant_row(me * nv + h * 128 + lane)) for h in range(nv // 128)]

    def rank_of(p):
        return odd if p == 0 else 1 - odd if p == blocks - 1 else p + 1

    def make(p, positive):
        r = rank_of(p)
        for h in range(nv // 128):
            base = 8 + p * own - 2
            out_ref[r, h * wide : (h + 1) * wide, :] = advect(
                lambda k: ext[h, base + k : base + k + wide, :], speeds[h], positive
            )
            if p == 0:
                out_ref[r, h * wide : h * wide + 4, :] = ext[h, 8:12, :]
            if p == blocks - 1:
                out_ref[r, h * wide + own : (h + 1) * wide, :] = ext[h, nx + 4 : nx + 8, :]

    def send(p):
        r = rank_of(p)
        return pltpu.make_async_copy(out_ref.at[r], out_hbm.at[r], out_sems.at[p])

    done = 0
    for p in range(parts):
        copies[p].wait()
        for h in range(nv // 128):
            ext[h, 8 + p * 128 : 8 + (p + 1) * 128, :] = f_ref[
                h * 128 : (h + 1) * 128, p * 128 : (p + 1) * 128
            ].T
        ready = blocks if p == parts - 1 else ((p + 1) * 128 - 4) // own
        for positive in (False, True):

            @pl.when(ahead == positive)
            def _(begin=done, positive=positive, ready=ready):
                for window in range(begin, ready):
                    make(window, positive)

        for window in range(done, ready):
            send(window).start()
        done = ready
    for window in range(blocks):
        send(window).wait()


def rate_kernel(blocks, rates_ref, kind_ref, rate_ref, edge_ref, ext):
    nx = kind_ref.shape[1]
    own = nx // blocks
    kinds = kind_ref[...]
    rate = jnp.zeros(kinds.shape, F32)
    for j in range(rates_ref.shape[1]):
        rate = jnp.where(kinds == j, rates_ref[0, j], rate)
    ext[0:8, :] = jnp.zeros((8, 128), F32)
    ext[8 : nx + 8, :] = jnp.broadcast_to(rate, (128, nx)).T
    ext[nx + 8 :, :] = jnp.zeros((8, 128), F32)
    spot = place(blocks)
    rate_ref[...] = ext[pl.ds(pl.multiple_of(spot * own, own), own + 16), :][6 : own + 10]
    edge_ref[...] = jnp.where(spot == 0, ext[8:16, :], ext[nx + 4 : nx + 12, :])


def edge_kernel(g_ref, rate_ref, token_ref, out_ref):
    blocks, rows, _ = g_ref.shape
    wide = rows // 2
    first = place(blocks) == 0
    for i in range(blocks):
        for h in range(2):
            n = 8 * i + 4 * h
            out_ref[n : n + 4, :] = jnp.where(
                first,
                g_ref[i, h * wide : h * wide + 4, :],
                g_ref[i, (h + 1) * wide - 4 : (h + 1) * wide, :],
            )
    out_ref[8 * blocks :, :] = rate_ref[...]


def mode_factor_kernel(table_hbm, sent_hbm, hi_hbm, lo_hbm, token_ref, hi_ref, lo_ref, table, sem, sems):
    token_ref[...] = jnp.zeros_like(token_ref)
    copy = pltpu.make_async_copy(table_hbm, table, sem)
    copy.start()
    copy.wait()
    row = lax.broadcasted_iota(jnp.int32, (D, 1), 0)

    def block(s, c, weight):
        near = 2 * D * s
        f = table[near : near + D, :] * table[pl.ds(4 * D + c, 1), :] - table[
            near + D : near + 2 * D, :
        ] * table[pl.ds(4 * D + K // (2 * D) + c, 1), :]
        if weight is not None:
            f = f * weight
        hi, lo = split(f)
        rows = pl.ds(pl.multiple_of(s * (K // 2) + c * D, D), D)
        hi_ref[rows, :] = hi
        lo_ref[rows, :] = lo

    def body(c, carry):
        block(0, c, None)
        block(1, c, None)
        return carry

    lax.fori_loop(0, K // (2 * D), body, 0)
    block(0, 0, jnp.where(row == 0, math.sqrt(0.5), 1.0))
    stores = [
        pltpu.make_async_copy(hi_ref, hi_hbm, sems.at[0]),
        pltpu.make_async_copy(lo_ref, lo_hbm, sems.at[1]),
    ]
    for store in stores:
        store.start()
    for store in stores:
        store.wait()


def factor_kernel(table_hbm, w_ref, edge_hbm, hi_ref, lo_ref, wp_ref, table, sem):
    copy = pltpu.make_async_copy(table_hbm, table, sem)
    copy.start()
    source = lax.broadcasted_iota(jnp.int32, (K, K), 0)
    target = lax.broadcasted_iota(jnp.int32, (K, K), 1)
    mode = jnp.where(target < K // 2, 2 * target, 2 * target + 1 - K)
    picks = jnp.where(source == mode, 1.0, 0.0).astype(BF16)
    wp_ref[...] = exact_dot(jnp.broadcast_to(w_ref[...], (8, K)), picks)
    copy.wait()

    def body(a, carry):
        f = table[0:B, :] * table[pl.ds(2 * B + a, 1), :] - table[B : 2 * B, :] * table[pl.ds(2 * B + A + a, 1), :]
        hi, lo = split(f)
        rows = pl.ds(pl.multiple_of(a * B, B), B)
        hi_ref[rows, :] = hi
        lo_ref[rows, :] = lo
        return carry

    lax.fori_loop(0, A, body, 0)


def collide_kernel(
    g_ref, e_ref, rate_in, hi_ref, lo_ref, wp_ref, thi_hbm, tlo_hbm,
    out_ref, a_ref, b_ref, r_ref, l_ref, c_ref, m_ref, s_ref, thi_ref, tlo_ref, sems,
):
    blocks, rows, _ = g_ref.shape
    wide = rows // 2
    own = wide - 4
    pad = 48
    half = K // 2
    chunks = H // 128
    lane = lax.broadcasted_iota(jnp.int32, (1, 128), 1)
    spot = place(blocks)
    loads = []
    for n in range(4):
        rows = slice(n // 2 * half, (n // 2 + 1) * half)
        source, target = ((thi_hbm, thi_ref), (tlo_hbm, tlo_ref))[n % 2]
        loads.append(pltpu.make_async_copy(source.at[rows, :], target.at[rows, :], sems.at[n]))
        loads[n].start()
    r_ref[...] = rate_in[...]

    def given(n):
        return g_ref[n // 2, (n % 2) * wide : (n % 2 + 1) * wide, :]

    for n in range(2 * chunks):
        b_ref[n, 0:wide, :] = given(n)

    def outer(first):
        for n in range(2 * chunks):
            mine = b_ref[n, 0:4, :] if first else b_ref[n, own:wide, :]
            other = e_ref[4 * n : 4 * n + 4, :]
            s_ref[n, 0:4, :] = other if first else mine
            s_ref[n, 4:8, :] = mine if first else other
            speed = jnp.abs(courant_row(lane + n * 128))
            new = advect(lambda k: s_ref[n, 2 + k : 6 + k, :], speed, n >= chunks)
            if first:
                b_ref[n, 0:4, :] = new
            else:
                b_ref[n, own:wide, :] = new
        if first:
            r_ref[0:2, :] = e_ref[8 * blocks + 2 : 8 * blocks + 4, :]
        else:
            r_ref[own + 2 : wide, :] = e_ref[8 * blocks : 8 * blocks + 2, :]

    @pl.when(spot == 0)
    def _():
        outer(True)

    @pl.when(spot == blocks - 1)
    def _():
        outer(False)

    def fold(c, up, down, at):
        count = up.shape[0]
        for part, first in ((up + down, c * 128), (up - down, H + c * 128)):
            hi, lo = split(part)
            l_ref[0:count, first : first + 128] = hi
            l_ref[at : at + count, first : first + 128] = lo

    def correction(count, at):
        for s in range(2):
            modes = slice(s * half, (s + 1) * half)
            left = l_ref[: 2 * at, s * H : (s + 1) * H]
            both = dot(left, hi_ref[:, modes])
            coef = both[:count] + both[at : at + count] + dot(left[:at], lo_ref[:, modes])[:count]
            hi, lo = split(coef * wp_ref[0:1, modes])
            m_ref[0:count, modes] = hi
            m_ref[at : at + count, modes] = lo
        for s in range(2):
            modes = slice(s * half, (s + 1) * half)
            right = m_ref[: 2 * at, modes]
            if count == wide:
                loads[2 * s].wait()
                loads[2 * s + 1].wait()
            back = dot(right, thi_ref[modes, :])
            c_ref[:count, s * H : (s + 1) * H] = (
                back[:count] + back[at : at + count] + dot(right[:at], tlo_ref[modes, :])[:count]
            )

    def corrections(count, c):
        even = c_ref[:count, c * 128 : (c + 1) * 128]
        odd = c_ref[:count, H + c * 128 : H + (c + 1) * 128]
        return even + odd, even - odd

    for c in range(chunks):
        down = mirrored(b_ref[2 * chunks - 1 - c, 0:wide, :])
        a_ref[chunks + c, 0:wide, :] = down
        fold(c, b_ref[c, 0:wide, :], down, pad)
    correction(wide, pad)
    rate = r_ref[...]
    for c in range(chunks):
        plus, minus = corrections(wide, c)
        a_ref[c, 0:wide, :] = b_ref[c, 0:wide, :] - rate * plus
        a_ref[chunks + c, 0:wide, :] = a_ref[chunks + c, 0:wide, :] - rate * minus
        speed = jnp.abs(courant_row(lane + c * 128))
        up = advect(lambda k: a_ref[c, 2 + k : 2 + k + own, :], speed, False)
        down = advect(lambda k: a_ref[chunks + c, 2 + k : 2 + k + own, :], speed, True)
        b_ref[c, 0:own, :] = up
        b_ref[chunks + c, 0:own, :] = down
        fold(c, up, down, own)
    correction(own, own)
    rate = r_ref[2 : own + 2, :]
    for c in range(chunks):
        plus, minus = corrections(own, c)
        n = 2 * chunks - 1 - c
        out_ref[c // 2, :, (c % 2) * 128 : (c % 2 + 1) * 128] = b_ref[c, 0:own, :] - rate * plus
        out_ref[n // 2, :, (n % 2) * 128 : (n % 2 + 1) * 128] = mirrored(
            b_ref[chunks + c, 0:own, :] - rate * minus
        )


def unflip_kernel(t_ref, out_hbm, out_ref, sems):
    blocks, own, _ = t_ref.shape
    odd = lax.rem(lax.axis_index("space"), 2)
    order = [odd] + [p + 1 for p in range(1, blocks - 1)] + [1 - odd]
    per = 128 // own
    copies = []
    for p in range(blocks // per):
        columns = slice(p * 128, (p + 1) * 128)
        rows = jnp.concatenate([t_ref[r] for r in order[p * per : (p + 1) * per]], axis=0)
        out_ref[:, columns] = rows.T
        copies.append(pltpu.make_async_copy(out_ref.at[:, columns], out_hbm.at[:, columns], sems.at[p]))
        copies[-1].start()
    for copy in copies:
        copy.wait()


def params(mib):
    return pltpu.CompilerParams(vmem_limit_bytes=mib * 1024 * 1024)


VMEM = pl.BlockSpec(memory_space=pltpu.VMEM)
SMEM = pl.BlockSpec(memory_space=pltpu.SMEM)
ANY = pl.BlockSpec(memory_space=pl.ANY)


def shards(distribution, cell_kind, type_rates, mode_weights):
    nv, nx = distribution.shape
    blocks = lax.axis_size("vel")
    slabs = lax.axis_size("space")
    own = nx // blocks
    wide = own + 4
    sent = pl.pallas_call(
        functools.partial(flip_kernel, blocks),
        out_shape=jax.ShapeDtypeStruct((blocks, nv // 128 * wide, 128), F32),
        in_specs=[ANY],
        out_specs=ANY,
        scratch_shapes=[
            pltpu.VMEM((nv, nx), F32),
            pltpu.VMEM((nv // 128, nx + 16, 128), F32),
            pltpu.VMEM((blocks, nv // 128 * wide, 128), F32),
            pltpu.SemaphoreType.DMA((nx // 128,)),
            pltpu.SemaphoreType.DMA((blocks,)),
        ],
        compiler_params=params(8),
        name="flip",
    )(pltpu.with_memory_space_constraint(distribution, pltpu.MemorySpace.HBM))
    got = lax.all_to_all(sent, "vel", 0, 0, tiled=True)
    rate, rate_edge = pl.pallas_call(
        functools.partial(rate_kernel, blocks),
        out_shape=(
            jax.ShapeDtypeStruct((wide, 128), F32),
            jax.ShapeDtypeStruct((8, 128), F32),
        ),
        in_specs=[SMEM, VMEM],
        out_specs=(VMEM, VMEM),
        scratch_shapes=[pltpu.VMEM((nx + 16, 128), F32)],
        compiler_params=params(8),
        name="rates",
    )(type_rates[None, :], cell_kind[None, :])
    *by_modes, token = pl.pallas_call(
        mode_factor_kernel,
        out_shape=(
            pltpu.MemorySpace.HBM((K, H), BF16),
            pltpu.MemorySpace.HBM((K, H), BF16),
            jax.ShapeDtypeStruct((8, 128), F32),
        ),
        in_specs=[ANY, ANY],
        out_specs=(ANY, ANY, VMEM),
        scratch_shapes=[
            pltpu.VMEM((K, H), BF16),
            pltpu.VMEM((K, H), BF16),
            pltpu.VMEM((4 * D + K // D, H), F32),
            pltpu.SemaphoreType.DMA,
            pltpu.SemaphoreType.DMA((2,)),
        ],
        compiler_params=params(16),
        name="mode_factors",
    )(jnp.asarray(mode_tables()), sent)
    edge = pl.pallas_call(
        edge_kernel,
        out_shape=jax.ShapeDtypeStruct((8 * blocks + 8, 128), F32),
        in_specs=[VMEM, VMEM, VMEM],
        out_specs=VMEM,
        compiler_params=params(8),
        name="edges",
    )(got, rate_edge, token)
    pairs = []
    for s in range(slabs):
        after = (s + 1) % slabs
        rank = 1 - s % 2
        pairs += [(rank * slabs + s, rank * slabs + after), (rank * slabs + after, rank * slabs + s)]
    edge_in = lax.ppermute(edge, ("vel", "space"), pairs)
    by_modes = [pltpu.with_memory_space_constraint(part, pltpu.MemorySpace.HBM) for part in by_modes]
    factors = pl.pallas_call(
        factor_kernel,
        out_shape=(
            jax.ShapeDtypeStruct((H, K), BF16),
            jax.ShapeDtypeStruct((H, K), BF16),
            jax.ShapeDtypeStruct((8, K), F32),
        ),
        in_specs=[ANY, VMEM, ANY],
        out_specs=(VMEM,) * 3,
        scratch_shapes=[pltpu.VMEM((2 * (A + B), K), F32), pltpu.SemaphoreType.DMA],
        compiler_params=params(12),
        name="factors",
    )(jnp.asarray(tables()), mode_weights[None, :], edge)
    back = pl.pallas_call(
        collide_kernel,
        out_shape=jax.ShapeDtypeStruct((blocks, own, nv), F32),
        in_specs=[VMEM] * 6 + [ANY] * 2,
        out_specs=VMEM,
        scratch_shapes=[
            pltpu.VMEM((V // 128, wide + 4, 128), F32),
            pltpu.VMEM((V // 128, wide + 4, 128), F32),
            pltpu.VMEM((wide, 128), F32),
            pltpu.VMEM((96, V), BF16),
            pltpu.VMEM((wide + 4, V), F32),
            pltpu.VMEM((96, K), BF16),
            pltpu.VMEM((V // 128, 8, 128), F32),
            pltpu.VMEM((K, H), BF16),
            pltpu.VMEM((K, H), BF16),
            pltpu.SemaphoreType.DMA((4,)),
        ],
        compiler_params=params(24),
        name="collide",
    )(got, edge_in, rate, *factors, *by_modes)
    result = lax.all_to_all(back, "vel", 0, 0, tiled=True)
    return pl.pallas_call(
        unflip_kernel,
        out_shape=jax.ShapeDtypeStruct((nv, nx), F32),
        in_specs=[VMEM],
        out_specs=ANY,
        scratch_shapes=[pltpu.VMEM((nv, nx), F32), pltpu.SemaphoreType.DMA((nx // 128,))],
        compiler_params=params(8),
        name="unflip",
    )(result)


def solution(mesh):
    return jax.shard_map(
        shards,
        mesh=mesh,
        in_specs=(P("vel", "space"), P("space"), P(), P()),
        out_specs=P("vel", "space"),
        check_vma=False,
    )
```
